512 devices in a mesh: run: 8 (over z), space: 64 (over x, y, core).
Axes of the slice: x: 4, y: 8, z: 8, core: 2. Of those that a mesh axis runs over, the one named last changes fastest.
Arguments:
- start_field: float32 [8, 64, 256, 512], P('run', 'space'), may hold values from -19 to 19
- viscosity: float32 [64, 256, 512], P('space'), may hold values from 0.5 to 1
- diffusivity: float32 [8], replicated, may hold values from 0.04 to 0.1
- velocity: float32 [8, 3], replicated, may hold values from -0.13 to 0.13
- assignment: int32 [8], replicated, may hold values from 0 to 7, each once
- child_order: int32 [7, 8], replicated, may hold values from 0 to 7, each once within a row
- keep_ranks: int32 [7], replicated, may hold values from 2 to 4
Outputs:
- root_factor: float32 [4, 64, 256, 512], P(None, 'space', 'run')
The draws below stay inside these ranges and needn't reach their ends.
Inputs may be any that keep to these rules, and one draw needn't show every extreme that they name: `assignment`: each sample appears once; runs read the first 8 entries. `child_order`: each row holds every number once.
All inputs are finite; a program needn't handle non-finite values.
Results may differ from the reference program's by a relative error of at most 0.0003.
Values sent between devices are 32-bit elements; how exact they have to be, the bound alone decides.
No kernel may reach another device: no remote copies, remote signals or barrier semaphores. Data moves between devices by JAX's collectives and lax.ppermute only.
A program may use at most 128 MiB of HBM per device.

```python
import math
import jax
import jax.numpy as jnp
from jax import lax

NY = 256
NZ = 512
STEPS = 4
SUBITERS = 3
SAMPLES = 8
RUNS = 8
NODES = 7
NX = 64
N_RUN = 8


def draw_start_field(key, part):
    shape_all = (RUNS, NX, NY, NZ)
    shape_common = (1, NX, NY, NZ)
    key_common = jax.random.fold_in(key, 11)
    key_own = jax.random.fold_in(key, 23)
    plane_ramp = jnp.arange(NX, dtype=jnp.float32) / max(NX - 1, 1)
    common_part = jnp.clip(jax.random.normal(key_common, shape_common, jnp.float32), -4.5, 4.5)
    own_part = jnp.clip(jax.random.normal(key_own, shape_all, jnp.float32), -4.5, 4.5)
    profile = jnp.exp(plane_ramp * math.log(3.0))
    rough_part = 0.8 * common_part + 0.6 * own_part
    return rough_part * profile[None, :, None, None]


def touch_ends(values, key, low, largest):
    longest = values.shape.index(max(values.shape))
    spots = []
    for shift in (0, 1):
        where = [jax.random.randint(jax.random.fold_in(key, axis), (), 0, length) for axis, length in enumerate(values.shape)]
        where[longest] = (where[longest] + shift) % values.shape[longest]
        spots.append(tuple(where))
    return values.at[spots[0]].set(low).at[spots[1]].set(largest)


def levels(rng, dims, split, least, largest):
    gain, own = 1.0, jax.random.fold_in(rng, 6)
    for dim, blocks in split:
        steps = jnp.exp(jax.random.uniform(jax.random.fold_in(own, dim), (blocks,), jnp.float32, least / len(split), largest / len(split)))
        gain = gain * jnp.repeat(steps, dims[dim] // blocks).reshape([-1 if axis == dim else 1 for axis in range(len(dims))])
    return gain


def setup_inputs(seed: int = 0) -> dict:
    seeds = jax.random.split(jax.random.key(seed), 8)
    return {
        "start_field": draw_start_field(jax.random.fold_in(seeds[7], 71), 0),
        "viscosity": jnp.clip(jnp.exp(math.log(1.0) - 0.6931472 * jax.random.uniform(seeds[1], (NX, NY, NZ), jnp.float32) ** levels(seeds[1], (NX, NY, NZ), ((0, 64),), -0.2, 0.2)), 0.5, 1.0),
        "diffusivity": jnp.clip(jnp.exp(jax.random.uniform(seeds[2], (SAMPLES,), jnp.float32, math.log(0.04), math.log(0.1))), 0.04, 0.1),
        "velocity": jnp.clip(jax.random.uniform(seeds[3], (SAMPLES, 3), jnp.float32, -0.13, 0.13), -0.13, 0.13),
        "assignment": jax.random.permutation(seeds[4], SAMPLES).astype(jnp.int32),
        "child_order": jax.vmap(lambda own: jax.random.permutation(own, 2 * STEPS))(jax.random.split(seeds[5], NODES)).reshape((NODES, 2 * STEPS)).astype(jnp.int32),
        "keep_ranks": touch_ends(jax.random.randint(seeds[6], (NODES,), 2, STEPS + 1), jax.random.fold_in(seeds[6], 1), 2, STEPS).astype(jnp.int32),
    }


EPS = 1e-06
EXACT = lax.Precision.HIGHEST

def neighbour(padded, direction, offset):
    window = [slice(1, -1), slice(1, -1), slice(1, -1)]
    window[direction] = slice(1 + offset, padded.shape[direction] - 1 + offset)
    return padded[tuple(window)]

def advance(ext_field, ext_visc, diffuse_rate, velocity_now):
    padded_state = jnp.pad(ext_field, ((0, 0), (1, 1), (1, 1)))
    padded_visc = jnp.pad(ext_visc, ((0, 0), (1, 1), (1, 1)))
    centre = padded_state[1:-1, 1:-1, 1:-1]
    visc_mid = padded_visc[1:-1, 1:-1, 1:-1]
    updated = centre
    for direction in range(3):
        ahead_cell = neighbour(padded_state, direction, 1)
        behind_cell = neighbour(padded_state, direction, -1)
        face_ahead = 0.5 * diffuse_rate * (visc_mid + neighbour(padded_visc, direction, 1))
        face_behind = 0.5 * diffuse_rate * (visc_mid + neighbour(padded_visc, direction, -1))
        speed_now = velocity_now[direction]
        updated = updated + face_ahead * (ahead_cell - centre) - face_behind * (centre - behind_cell)
        updated = updated - jnp.maximum(speed_now, 0.0) * (centre - behind_cell) - jnp.minimum(speed_now, 0.0) * (ahead_cell - centre)
    return updated

def leading(gram_matrix, kept_rank, snap_width):
    full_size = 2 * snap_width
    row_ids = jnp.arange(full_size, dtype=jnp.float32)[:, None]
    col_ids = jnp.arange(snap_width, dtype=jnp.float32)[None, :]
    start_basis = jnp.cos(math.pi * (row_ids + 0.5) * (col_ids + 0.5) / full_size) * math.sqrt(1.0 / snap_width)
    live_cols = (jnp.arange(snap_width, dtype=jnp.int32) < kept_rank).astype(jnp.float32)
    current = start_basis * live_cols[None, :]
    for sweep_index in range(SUBITERS):
        image_cols = jnp.dot(gram_matrix, current, precision=EXACT) * live_cols[None, :]
        inner_gram = jnp.dot(image_cols.T, image_cols, precision=EXACT) + jnp.diag(1.0 - live_cols)
        factor_low = jnp.linalg.cholesky(inner_gram)
        current = jax.scipy.linalg.solve_triangular(factor_low, image_cols.T, lower=True).T
    return current

def reference(start_field, viscosity, diffusivity, velocity, assignment, child_order, keep_ranks):
    cell_count = NX * NY * NZ
    visc_ext = jnp.pad(viscosity, ((1, 1), (0, 0), (0, 0)))

    def leaf_factor(run_slot):
        chosen = assignment[run_slot]
        diffuse_rate = diffusivity[chosen]
        velocity_now = velocity[chosen]
        current = start_field[run_slot]
        snapshots = []
        for step_index in range(STEPS):
            current = advance(jnp.pad(current, ((1, 1), (0, 0), (0, 0))), visc_ext, diffuse_rate, velocity_now)
            snapshots.append(current)
        stacked = jnp.stack(snapshots).reshape(STEPS, cell_count)
        squares = lax.optimization_barrier(jnp.sum(stacked * stacked, axis=1))
        return stacked / jnp.sqrt(squares / cell_count + EPS)[:, None]

    def node_factor(tree_level, position):
        if tree_level == 0:
            return leaf_factor(position)
        lower_side = node_factor(tree_level - 1, 2 * position)
        upper_side = node_factor(tree_level - 1, 2 * position + 1)
        node_id = N_RUN - (N_RUN >> tree_level - 1) + position
        row_perm = child_order[node_id].astype(jnp.int32)
        stacked = jnp.take(jnp.concatenate([lower_side, upper_side], axis=0), row_perm, axis=0)
        gram_matrix = jnp.dot(stacked, stacked.T, precision=EXACT) / cell_count
        basis_now = leading(gram_matrix, keep_ranks[node_id], STEPS)
        return jnp.dot(basis_now.T, stacked, precision=EXACT)
    levels_total = N_RUN.bit_length() - 1
    root_rows = node_factor(levels_total, 0)
    return root_rows.reshape(STEPS, NX, NY, NZ)
```

```python
import math

import jax
import jax.numpy as jnp
from jax import lax
from jax.experimental import pallas as pl
from jax.experimental.pallas import tpu as pltpu
from jax.sharding import Mesh, PartitionSpec as P

STEPS = 4
SUBITERS = 3
EPS = 1e-06
RUNS = 8
NY = 256
NZ = 512
NX = 64
BLOCK = NY // RUNS
HALO = STEPS
EXT = BLOCK + 2 * HALO
CELLS = NX * NY * NZ
EXACT = lax.Precision.HIGHEST
SPACE = ("x", "y", "core")
VMEM = pl.BlockSpec(memory_space=pltpu.VMEM)
SMEM = pl.BlockSpec(memory_space=pltpu.SMEM)


def sub_iota(shape):
    return lax.broadcasted_iota(jnp.int32, shape, 0)


def lane_iota(shape):
    return lax.broadcasted_iota(jnp.int32, shape, 1)


def params(limit=40 << 20):
    return pltpu.CompilerParams(vmem_limit_bytes=limit)


def blocks_kernel(field_ref, visc_ref, out_ref, visc_out):
    run = lax.axis_index("run")
    low = sub_iota((8, NZ)) < 4
    zero = jnp.zeros((8, NZ), jnp.float32)
    tiles = NY // 8

    def shifted(before, after):
        return pltpu.roll(jnp.where(low, after, before), 4, 0)

    before = zero
    for m in range(tiles + 1):
        after = field_ref[0, 0, 8 * m : 8 * m + 8, :] if m < tiles else zero
        tile = shifted(before, after)
        before = after
        for q in range(RUNS):
            j = m - 4 * q
            if 0 <= j <= 4:
                out_ref[q, 8 * j : 8 * j + 8, :] = tile
    for j in range(5):
        m = 4 * run + j
        prev_at = pl.multiple_of(8 * jnp.maximum(m - 1, 0), 8)
        next_at = pl.multiple_of(8 * jnp.minimum(m, tiles - 1), 8)
        prev = jnp.where(m > 0, visc_ref[0, pl.ds(prev_at, 8), :], 0.0)
        nxt = jnp.where(m < tiles, visc_ref[0, pl.ds(next_at, 8), :], 0.0)
        visc_out[0, 8 * j : 8 * j + 8, :] = shifted(prev, nxt)


def row_blocks(field, visc):
    return pl.pallas_call(
        blocks_kernel,
        out_shape=(
            jax.ShapeDtypeStruct((RUNS, EXT, NZ), jnp.float32),
            jax.ShapeDtypeStruct((1, EXT, NZ), jnp.float32),
        ),
        in_specs=[VMEM, VMEM],
        out_specs=(VMEM, VMEM),
        compiler_params=params(),
        cost_estimate=pl.CostEstimate(flops=200000, bytes_accessed=2000000, transcendentals=0),
        name="row_blocks",
    )(field, visc)


def step_kernel(last, diff_ref, vel_ref, assign_ref, u_ref, sib_ref, cross_ref, v_ref, vs_ref, vc_ref, *outs):
    run = lax.axis_index("run")
    even = lax.axis_index("core") == 0
    shape = (EXT, NZ)
    row = sub_iota(shape) + (BLOCK * run - HALO)
    inside = (row >= 0) & (row < NY)
    col = lane_iota(shape)
    first_col = col == 0
    last_col = col == NZ - 1
    v = v_ref[0]
    vs = vs_ref[0]
    vc = vc_ref[0]

    def ahead_row(a):
        return pltpu.roll(a, EXT - 1, 0)

    def behind_row(a):
        return pltpu.roll(a, 1, 0)

    def ahead_col(a):
        return jnp.where(last_col, 0.0, pltpu.roll(a, NZ - 1, 1))

    def behind_col(a):
        return jnp.where(first_col, 0.0, pltpu.roll(a, 1, 1))

    c_sib = 0.5 * (v + vs)
    c_cross = 0.5 * (v + vc)
    c_yp = 0.5 * (v + ahead_row(v))
    c_ym = 0.5 * (v + behind_row(v))
    c_zp = 0.5 * (v + ahead_col(v))
    c_zm = 0.5 * (v + behind_col(v))
    for q in range(RUNS):
        s = assign_ref[q]
        kappa = diff_ref[s]
        ups = [-jnp.minimum(vel_ref[s, d], 0.0) for d in range(3)]
        downs = [jnp.maximum(vel_ref[s, d], 0.0) for d in range(3)]
        u = u_ref[q]
        w_sib = jnp.where(even, ups[0], downs[0])
        w_cross = jnp.where(even, downs[0], ups[0])
        new = u + (kappa * c_sib + w_sib) * (sib_ref[q] - u)
        new = new + (kappa * c_cross + w_cross) * (cross_ref[q] - u)
        new = new + (kappa * c_yp + ups[1]) * (ahead_row(u) - u)
        new = new + (kappa * c_ym + downs[1]) * (behind_row(u) - u)
        new = new + (kappa * c_zp + ups[2]) * (ahead_col(u) - u)
        new = new + (kappa * c_zm + downs[2]) * (behind_col(u) - u)
        new = jnp.where(inside, new, 0.0)
        if not last:
            outs[0][q] = new
        outs[-1][q] = pltpu.roll(new, EXT - HALO, 0)[:BLOCK]


def advance(last, coefs, state, sib, cross, visc, visc_sib, visc_cross):
    core = jax.ShapeDtypeStruct((RUNS, BLOCK, NZ), jnp.float32)
    full = jax.ShapeDtypeStruct((RUNS, EXT, NZ), jnp.float32)
    out = (core,) if last else (full, core)

    def body(*refs):
        step_kernel(last, *refs)

    return pl.pallas_call(
        body,
        out_shape=out,
        in_specs=[SMEM, SMEM, SMEM] + [VMEM] * 6,
        out_specs=tuple(VMEM for _ in out),
        compiler_params=params(),
        cost_estimate=pl.CostEstimate(flops=6000000, bytes_accessed=4000000, transcendentals=0),
        name="step_last" if last else "step",
    )(*coefs, state, sib, cross, visc, visc_sib, visc_cross)


def merge(x, y, width):
    sub = sub_iota((8, 128))
    pick = (sub & width) == 0
    keep = jnp.where(pick, x, y)
    give = jnp.where(pick, y, x)
    if width == 4:
        moved = pltpu.roll(give, 4, 0)
    else:
        moved = jnp.where(pick, pltpu.roll(give, 8 - width, 0), pltpu.roll(give, width, 0))
    return keep + moved


def gram_kernel(group, last, *refs):
    cores = refs[: group + 1]
    prev_ref = refs[group + 1] if group else None
    out_ref = refs[-1]
    mine = cores[group]
    lane = lane_iota((8, 128))
    packed = prev_ref[...] if group else jnp.zeros((8, 128), jnp.float32)
    for other in range(group + 1):
        theirs = cores[other]
        for half in range(2):
            accs = tuple(jnp.zeros((8, 128), jnp.float32) for _ in range(32))

            def body(i, accs, theirs=theirs, half=half):
                rows = pl.ds(pl.multiple_of(8 * i, 8), 8)
                accs = list(accs)
                for l in range(NZ // 128):
                    cols = slice(128 * l, 128 * l + 128)
                    a = [mine[4 * half + k, rows, cols] for k in range(4)]
                    for b in range(8):
                        t = theirs[b, rows, cols]
                        for k in range(4):
                            accs[8 * k + b] = accs[8 * k + b] + a[k] * t
                return tuple(accs)

            accs = lax.fori_loop(0, BLOCK // 8, body, accs)
            for k in range(4):
                level = list(accs[8 * k : 8 * k + 8])
                for width in (4, 2, 1):
                    count = len(level) // 2
                    level = [merge(level[i], level[i + count], width) for i in range(count)]
                total = jnp.sum(level[0], axis=1, keepdims=True)
                at = 32 * other + 8 * group + 4 * half + k
                packed = jnp.where(lane == at, total, packed)
    if last:
        for i in range(RUNS):
            out_ref[i] = packed
    else:
        out_ref[...] = packed


def gram(cores, prev, last):
    group = len(cores) - 1
    shape = (RUNS, 8, 128) if last else (8, 128)
    args = list(cores) + ([prev] if group else [])

    def body(*refs):
        gram_kernel(group, last, *refs)

    return pl.pallas_call(
        body,
        out_shape=jax.ShapeDtypeStruct(shape, jnp.float32),
        in_specs=[VMEM] * len(args),
        out_specs=VMEM,
        compiler_params=params(),
        cost_estimate=pl.CostEstimate(flops=2200000 * (group + 1), bytes_accessed=600000 * (group + 1), transcendentals=0),
        name=f"gram{group}",
    )(*args)


def spread_kernel(in_ref, out_ref):
    total = in_ref[0]
    for i in range(1, RUNS):
        total = total + in_ref[i]
    for i in range(RUNS):
        out_ref[i] = total


def spread(parts):
    return pl.pallas_call(
        spread_kernel,
        out_shape=jax.ShapeDtypeStruct(parts.shape, jnp.float32),
        in_specs=[VMEM],
        out_specs=VMEM,
        name="spread",
    )(parts)


def dot(a, b):
    return jnp.dot(a, b, precision=EXACT, preferred_element_type=jnp.float32)


def dct():
    size = 2 * STEPS
    return [
        [math.sqrt(1.0 / STEPS) * math.cos(math.pi * (i + 0.5) * (j + 0.5) / size) for j in range(STEPS)]
        for i in range(size)
    ]


def sublane_sum(a):
    for width in (4, 2, 1):
        a = a + pltpu.roll(a, width, 0)
    return a


def level_basis(gram_now, nodes, first_node, order_ref, keep_ref):
    shape = (8, 128)
    sub = sub_iota(shape)
    lane = lane_iota(shape) & (nodes - 1)
    table = dct()
    basis = [jnp.zeros(shape, jnp.float32) for _ in range(STEPS)]
    live = [jnp.zeros(shape, jnp.float32) for _ in range(STEPS)]
    for k in range(nodes):
        node = first_node + k
        here = lane == k
        for c in range(STEPS):
            flag = jnp.where(keep_ref[node] > c, 1.0, 0.0)
            live[c] = jnp.where(here, flag, live[c])
        for i in range(2 * STEPS):
            spot = here & (sub == order_ref[node, i])
            for c in range(STEPS):
                basis[c] = jnp.where(spot, table[i][c], basis[c])
    basis = [z * m for z, m in zip(basis, live)]
    cols = []
    for j in range(8):
        col = jnp.zeros(shape, jnp.float32)
        for k in range(nodes):
            piece = gram_now[8 * k : 8 * k + 8, 8 * k + j : 8 * k + j + 1]
            col = jnp.where(lane == k, piece, col)
        cols.append(col)
    for _ in range(SUBITERS):
        image = []
        for c in range(STEPS):
            total = cols[0] * basis[c][0:1, :]
            for j in range(1, 8):
                total = total + cols[j] * basis[c][j : j + 1, :]
            image.append(total * live[c])
        inner = {}
        for a in range(STEPS):
            for b in range(a + 1):
                inner[a, b] = sublane_sum(image[a] * image[b])
            inner[a, a] = inner[a, a] + (1.0 - live[a])
        low = {}
        inv = []
        for b in range(STEPS):
            pivot = inner[b, b]
            for k in range(b):
                pivot = pivot - low[b, k] * low[b, k]
            root = 1.0 / jnp.sqrt(pivot)
            inv.append(root)
            for a in range(b + 1, STEPS):
                entry = inner[a, b]
                for k in range(b):
                    entry = entry - low[a, k] * low[b, k]
                low[a, b] = entry * root
        fresh = []
        for a in range(STEPS):
            value = image[a]
            for k in range(a):
                value = value - low[a, k] * fresh[k]
            fresh.append(value * inv[a])
        basis = fresh
    return basis


def weights(basis, nodes):
    lane = lane_iota((8, 128))
    rows = []
    for k in range(nodes):
        block = jnp.zeros((8, 128), jnp.float32)
        for c in range(STEPS):
            block = jnp.where(lane == STEPS * k + c, basis[c][:, k : k + 1], block)
        rows.append(block)
    return jnp.concatenate(rows, axis=0) if nodes > 1 else rows[0]


def finish_kernel(order_ref, keep_ref, part_ref, c0, c1, c2, c3, out_ref, w_ref):
    packed = part_ref[0]
    for i in range(1, RUNS):
        packed = packed + part_ref[i]
    size = RUNS * STEPS
    raw = jnp.concatenate(
        [packed if j == 0 else pltpu.roll(packed, 128 - size * j, 1) for j in range(STEPS)], axis=0
    )
    sub = sub_iota((size, 128))
    lane = lane_iota((size, 128))
    raw = jnp.where(lane < size, raw, 0.0)
    square = jnp.concatenate([raw, jnp.zeros((128 - size, 128), jnp.float32)], axis=0)
    mirror = square.T[:size, :]
    raw = jnp.where((sub >> 3) <= (lane >> 3), raw, mirror)
    source = 8 * (sub & 3) + (sub >> 2)
    perm = jnp.where(lane == source, 1.0, 0.0)
    rows = dot(perm[:, :size], raw)
    target = 8 * (lane & 3) + (lane >> 2)
    perm_t = jnp.where((sub == target) & (lane < size), 1.0, 0.0)
    full = dot(rows[:, :size], perm_t)
    diag = jnp.where(sub == lane, full, 0.0)
    mu_col = jnp.sum(diag, axis=1, keepdims=True) / CELLS
    mu_row = jnp.sum(diag, axis=0, keepdims=True) / CELLS
    scale_col = 1.0 / jnp.sqrt(mu_col + EPS)
    scale_row = 1.0 / jnp.sqrt(mu_row + EPS)
    gram_now = full * scale_col * scale_row / CELLS
    nodes = RUNS // 2
    first_node = 0
    total = None
    while nodes:
        basis = level_basis(gram_now, nodes, first_node, order_ref, keep_ref)
        w = weights(basis, nodes)
        rows_now = 8 * nodes
        total = w if total is None else dot(total[:, :rows_now], w)
        if nodes > 1:
            half = dot(gram_now[:, :rows_now], w)
            w_t = jnp.concatenate([w, jnp.zeros((128 - rows_now, 128), jnp.float32)], axis=0).T
            gram_now = dot(w_t[: STEPS * nodes, :rows_now], half)
        first_node += nodes
        nodes //= 2
    total = total * scale_col
    for c in range(STEPS):
        w_ref[c] = jnp.broadcast_to(total[:, c : c + 1], (size, 128))
    cores = (c0, c1, c2, c3)
    for l in range(NZ // 128):
        cols = slice(128 * l, 128 * l + 128)
        for i in range(BLOCK // 8):
            rws = slice(8 * i, 8 * i + 8)
            accs = [None] * STEPS
            for q in range(RUNS):
                for t in range(STEPS):
                    x = cores[t][q, rws, cols]
                    k = STEPS * q + t
                    for c in range(STEPS):
                        term = w_ref[c, k : k + 1, :] * x
                        accs[c] = term if accs[c] is None else accs[c] + term
            for c in range(STEPS):
                out_ref[c, 0, rws, cols] = accs[c]


def finish(order, keep, parts, cores):
    return pl.pallas_call(
        finish_kernel,
        out_shape=jax.ShapeDtypeStruct((STEPS, 1, BLOCK, NZ), jnp.float32),
        in_specs=[SMEM, SMEM] + [VMEM] * 5,
        out_specs=VMEM,
        scratch_shapes=[pltpu.VMEM((STEPS, RUNS * STEPS, 128), jnp.float32)],
        compiler_params=params(),
        cost_estimate=pl.CostEstimate(flops=5000000, bytes_accessed=2400000, transcendentals=0),
        name="finish",
    )(order, keep, parts, *cores)


def local(start_field, viscosity, diffusivity, velocity, assignment, child_order, keep_ranks):
    coefs = (diffusivity, velocity, assignment)
    sibling = [(i, i ^ 1) for i in range(NX)]
    crossing = [(i, i + 1) for i in range(1, NX - 1, 2)] + [(i + 1, i) for i in range(1, NX - 1, 2)]
    blocks, visc = row_blocks(start_field, viscosity)
    state = lax.all_to_all(blocks, "run", 0, 0)
    send = jnp.concatenate([state, visc], axis=0)
    cores = []
    packed = None
    for step in range(STEPS):
        cross = lax.ppermute(send, SPACE, crossing)
        sib = lax.ppermute(send, SPACE, sibling)
        if cores:
            packed = gram(cores, packed, False)
        if step == 0:
            visc_sib, visc_cross = sib[RUNS:], cross[RUNS:]
        last = step == STEPS - 1
        result = advance(last, coefs, state, sib, cross, visc, visc_sib, visc_cross)
        cores.append(result[-1])
        state = send = result[0]
    parts = gram(cores, packed, True)
    parts = spread(lax.all_to_all(parts, ("x", "core"), 0, 0))
    parts = spread(lax.all_to_all(parts, "y", 0, 0))
    parts = lax.all_to_all(parts, "run", 0, 0)
    return finish(child_order, keep_ranks, parts, cores)


def solution(mesh):
    fine = Mesh(mesh.devices.reshape(8, 4, 8, 2), ("run", "x", "y", "core"))
    in_specs = (P("run", SPACE, None, None), P(SPACE, None, None), P(), P(), P(), P(), P())
    out_specs = P(None, SPACE, "run", None)
    return jax.shard_map(local, mesh=fine, in_specs=in_specs, out_specs=out_specs, check_vma=False)
```

```python
import math

import jax
import jax.numpy as jnp
from jax import lax
from jax.experimental import pallas as pl
from jax.experimental.pallas import tpu as pltpu
from jax.sharding import Mesh, PartitionSpec as P

STEPS = 4
SUBITERS = 3
EPS = 1e-06
RUNS = 8
NY = 256
NZ = 512
NX = 64
BLOCK = NY // RUNS
HALO = STEPS
EXT = BLOCK + 2 * HALO
CELLS = NX * NY * NZ
EXACT = lax.Precision.HIGHEST
SPACE = ("x", "y", "core")
GROUPS = ((0, 4), (4, 8))
FIRST = 16
SECOND = 32
VMEM = pl.BlockSpec(memory_space=pltpu.VMEM)
SMEM = pl.BlockSpec(memory_space=pltpu.SMEM)


def sub_iota(shape):
    return lax.broadcasted_iota(jnp.int32, shape, 0)


def lane_iota(shape):
    return lax.broadcasted_iota(jnp.int32, shape, 1)


def params(limit=40 << 20):
    return pltpu.CompilerParams(vmem_limit_bytes=limit)


def blocks_kernel(field_ref, visc_ref, out_ref, visc_out):
    run = lax.axis_index("run")
    low = sub_iota((8, NZ)) < 4
    zero = jnp.zeros((8, NZ), jnp.float32)
    tiles = NY // 8

    def shifted(before, after):
        return pltpu.roll(jnp.where(low, after, before), 4, 0)

    before = zero
    for m in range(tiles + 1):
        after = field_ref[0, 0, 8 * m : 8 * m + 8, :] if m < tiles else zero
        tile = shifted(before, after)
        before = after
        for q in range(RUNS):
            j = m - 4 * q
            if 0 <= j <= 4:
                out_ref[q, 8 * j : 8 * j + 8, :] = tile
    for j in range(5):
        m = 4 * run + j
        prev_at = pl.multiple_of(8 * jnp.maximum(m - 1, 0), 8)
        next_at = pl.multiple_of(8 * jnp.minimum(m, tiles - 1), 8)
        prev = jnp.where(m > 0, visc_ref[0, pl.ds(prev_at, 8), :], 0.0)
        nxt = jnp.where(m < tiles, visc_ref[0, pl.ds(next_at, 8), :], 0.0)
        visc_out[0, 8 * j : 8 * j + 8, :] = shifted(prev, nxt)


def row_blocks(field, visc):
    return pl.pallas_call(
        blocks_kernel,
        out_shape=(
            jax.ShapeDtypeStruct((RUNS, EXT, NZ), jnp.float32),
            jax.ShapeDtypeStruct((1, EXT, NZ), jnp.float32),
        ),
        in_specs=[VMEM, VMEM],
        out_specs=(VMEM, VMEM),
        compiler_params=params(),
        cost_estimate=pl.CostEstimate(flops=200000, bytes_accessed=2000000, transcendentals=0),
        name="row_blocks",
    )(field, visc)


def assemble_kernel(state_ref, visc_ref, *outs):
    for g, (start, stop) in enumerate(GROUPS):
        for q in range(start, stop):
            outs[g][q - start] = state_ref[q]
    outs[0][GROUPS[0][1]] = visc_ref[0]


def assemble(state, visc):
    shapes = [stop - start for start, stop in GROUPS]
    shapes[0] += 1
    return pl.pallas_call(
        assemble_kernel,
        out_shape=tuple(jax.ShapeDtypeStruct((n, EXT, NZ), jnp.float32) for n in shapes),
        in_specs=[VMEM, VMEM],
        out_specs=tuple(VMEM for _ in shapes),
        compiler_params=params(),
        cost_estimate=pl.CostEstimate(flops=0, bytes_accessed=1400000, transcendentals=0),
        name="assemble",
    )(state, visc)


def step_kernel(last, start, stop, diff_ref, vel_ref, assign_ref, u_ref, sib_ref, cross_ref, v_ref, vs_ref, vc_ref, *outs):
    run = lax.axis_index("run")
    even = lax.axis_index("core") == 0
    shape = (EXT, NZ)
    row = sub_iota(shape) + (BLOCK * run - HALO)
    inside = (row >= 0) & (row < NY)
    col = lane_iota(shape)
    first_col = col == 0
    last_col = col == NZ - 1
    v = v_ref[0]
    vs = vs_ref[GROUPS[0][1]]
    vc = vc_ref[GROUPS[0][1]]

    def ahead_row(a):
        return pltpu.roll(a, EXT - 1, 0)

    def behind_row(a):
        return pltpu.roll(a, 1, 0)

    def ahead_col(a):
        return jnp.where(last_col, 0.0, pltpu.roll(a, NZ - 1, 1))

    def behind_col(a):
        return jnp.where(first_col, 0.0, pltpu.roll(a, 1, 1))

    c_sib = 0.5 * (v + vs)
    c_cross = 0.5 * (v + vc)
    c_yp = 0.5 * (v + ahead_row(v))
    c_ym = 0.5 * (v + behind_row(v))
    c_zp = 0.5 * (v + ahead_col(v))
    c_zm = 0.5 * (v + behind_col(v))
    for q in range(stop - start):
        s = assign_ref[start + q]
        kappa = diff_ref[s]
        ups = [-jnp.minimum(vel_ref[s, d], 0.0) for d in range(3)]
        downs = [jnp.maximum(vel_ref[s, d], 0.0) for d in range(3)]
        u = u_ref[q]
        w_sib = jnp.where(even, ups[0], downs[0])
        w_cross = jnp.where(even, downs[0], ups[0])
        new = u + (kappa * c_sib + w_sib) * (sib_ref[q] - u)
        new = new + (kappa * c_cross + w_cross) * (cross_ref[q] - u)
        new = new + (kappa * c_yp + ups[1]) * (ahead_row(u) - u)
        new = new + (kappa * c_ym + downs[1]) * (behind_row(u) - u)
        new = new + (kappa * c_zp + ups[2]) * (ahead_col(u) - u)
        new = new + (kappa * c_zm + downs[2]) * (behind_col(u) - u)
        new = jnp.where(inside, new, 0.0)
        if not last:
            outs[0][q] = new
        outs[-1][q] = pltpu.roll(new, EXT - HALO, 0)[:BLOCK]


def advance(last, group, coefs, state, sib, cross, visc, visc_sib, visc_cross):
    start, stop = group
    core = jax.ShapeDtypeStruct((stop - start, BLOCK, NZ), jnp.float32)
    full = jax.ShapeDtypeStruct((stop - start, EXT, NZ), jnp.float32)
    out = (core,) if last else (full, core)

    def body(*refs):
        step_kernel(last, start, stop, *refs)

    return pl.pallas_call(
        body,
        out_shape=out,
        in_specs=[SMEM, SMEM, SMEM] + [VMEM] * 6,
        out_specs=tuple(VMEM for _ in out),
        compiler_params=params(),
        cost_estimate=pl.CostEstimate(
            flops=750000 * (stop - start), bytes_accessed=500000 * (stop - start), transcendentals=0
        ),
        name="step_last" if last else "step",
    )(*coefs, state, sib, cross, visc, visc_sib, visc_cross)


def merge(x, y, width):
    sub = sub_iota((8, 128))
    pick = (sub & width) == 0
    keep = jnp.where(pick, x, y)
    give = jnp.where(pick, y, x)
    if width == 4:
        moved = pltpu.roll(give, 4, 0)
    else:
        moved = jnp.where(pick, pltpu.roll(give, 8 - width, 0), pltpu.roll(give, width, 0))
    return keep + moved


def by_run(refs):
    return [refs[g].at[q - start] for g, (start, stop) in enumerate(GROUPS) for q in range(start, stop)]


def gram_kernel(group, last, *refs):
    pieces = len(GROUPS)
    cores = [by_run(refs[pieces * t : pieces * t + pieces]) for t in range(group + 1)]
    prev_ref = refs[pieces * (group + 1)] if group else None
    out_ref = refs[-1]
    mine = cores[group]
    lane = lane_iota((8, 128))
    packed = prev_ref[...] if group else jnp.zeros((8, 128), jnp.float32)
    for other in range(group + 1):
        theirs = cores[other]
        for half in range(2):
            accs = tuple(jnp.zeros((8, 128), jnp.float32) for _ in range(32))

            def body(i, accs, theirs=theirs, half=half):
                rows = pl.ds(pl.multiple_of(8 * i, 8), 8)
                accs = list(accs)
                for l in range(NZ // 128):
                    cols = slice(128 * l, 128 * l + 128)
                    a = [mine[4 * half + k][rows, cols] for k in range(4)]
                    for b in range(8):
                        t = theirs[b][rows, cols]
                        for k in range(4):
                            accs[8 * k + b] = accs[8 * k + b] + a[k] * t
                return tuple(accs)

            accs = lax.fori_loop(0, BLOCK // 8, body, accs)
            for k in range(4):
                level = list(accs[8 * k : 8 * k + 8])
                for width in (4, 2, 1):
                    count = len(level) // 2
                    level = [merge(level[i], level[i + count], width) for i in range(count)]
                total = jnp.sum(level[0], axis=1, keepdims=True)
                at = 32 * other + 8 * group + 4 * half + k
                packed = jnp.where(lane == at, total, packed)
    if last:
        for i in range(FIRST):
            out_ref[i] = packed
    else:
        out_ref[...] = packed


def gram(cores, prev, last):
    group = len(cores) - 1
    shape = (FIRST, 8, 128) if last else (8, 128)
    args = [piece for core in cores for piece in core] + ([prev] if group else [])

    def body(*refs):
        gram_kernel(group, last, *refs)

    return pl.pallas_call(
        body,
        out_shape=jax.ShapeDtypeStruct(shape, jnp.float32),
        in_specs=[VMEM] * len(args),
        out_specs=VMEM,
        compiler_params=params(),
        cost_estimate=pl.CostEstimate(flops=2200000 * (group + 1), bytes_accessed=600000 * (group + 1), transcendentals=0),
        name=f"gram{group}",
    )(*args)


def spread_kernel(in_ref, out_ref):
    total = in_ref[0]
    for i in range(1, FIRST):
        total = total + in_ref[i]
    for i in range(SECOND):
        out_ref[i] = total


def spread(parts):
    return pl.pallas_call(
        spread_kernel,
        out_shape=jax.ShapeDtypeStruct((SECOND, 8, 128), jnp.float32),
        in_specs=[VMEM],
        out_specs=VMEM,
        compiler_params=params(),
        name="spread",
    )(parts)


def dot(a, b):
    return jnp.dot(a, b, precision=EXACT, preferred_element_type=jnp.float32)


def dct():
    size = 2 * STEPS
    return [
        [math.sqrt(1.0 / STEPS) * math.cos(math.pi * (i + 0.5) * (j + 0.5) / size) for j in range(STEPS)]
        for i in range(size)
    ]


def sublane_sum(a):
    for width in (4, 2, 1):
        a = a + pltpu.roll(a, width, 0)
    return a


def level_basis(gram_now, nodes, first_node, order_ref, keep_ref):
    shape = (8, 128)
    sub = sub_iota(shape)
    lane = lane_iota(shape) & (nodes - 1)
    table = dct()
    basis = [jnp.zeros(shape, jnp.float32) for _ in range(STEPS)]
    live = [jnp.zeros(shape, jnp.float32) for _ in range(STEPS)]
    for k in range(nodes):
        node = first_node + k
        here = lane == k
        for c in range(STEPS):
            flag = jnp.where(keep_ref[node] > c, 1.0, 0.0)
            live[c] = jnp.where(here, flag, live[c])
        for i in range(2 * STEPS):
            spot = here & (sub == order_ref[node, i])
            for c in range(STEPS):
                basis[c] = jnp.where(spot, table[i][c], basis[c])
    basis = [z * m for z, m in zip(basis, live)]
    cols = []
    for j in range(8):
        col = jnp.zeros(shape, jnp.float32)
        for k in range(nodes):
            piece = gram_now[8 * k : 8 * k + 8, 8 * k + j : 8 * k + j + 1]
            col = jnp.where(lane == k, piece, col)
        cols.append(col)
    for _ in range(SUBITERS):
        image = []
        for c in range(STEPS):
            total = cols[0] * basis[c][0:1, :]
            for j in range(1, 8):
                total = total + cols[j] * basis[c][j : j + 1, :]
            image.append(total * live[c])
        inner = {}
        for a in range(STEPS):
            for b in range(a + 1):
                inner[a, b] = sublane_sum(image[a] * image[b])
            inner[a, a] = inner[a, a] + (1.0 - live[a])
        low = {}
        inv = []
        for b in range(STEPS):
            pivot = inner[b, b]
            for k in range(b):
                pivot = pivot - low[b, k] * low[b, k]
            root = 1.0 / jnp.sqrt(pivot)
            inv.append(root)
            for a in range(b + 1, STEPS):
                entry = inner[a, b]
                for k in range(b):
                    entry = entry - low[a, k] * low[b, k]
                low[a, b] = entry * root
        fresh = []
        for a in range(STEPS):
            value = image[a]
            for k in range(a):
                value = value - low[a, k] * fresh[k]
            fresh.append(value * inv[a])
        basis = fresh
    return basis


def weights(basis, nodes):
    lane = lane_iota((8, 128))
    rows = []
    for k in range(nodes):
        block = jnp.zeros((8, 128), jnp.float32)
        for c in range(STEPS):
            block = jnp.where(lane == STEPS * k + c, basis[c][:, k : k + 1], block)
        rows.append(block)
    return jnp.concatenate(rows, axis=0) if nodes > 1 else rows[0]


def finish_kernel(order_ref, keep_ref, part_ref, *refs):
    out_ref, w_ref = refs[-2:]
    pieces = len(GROUPS)
    cores = [by_run(refs[pieces * t : pieces * t + pieces]) for t in range(STEPS)]
    packed = part_ref[0]
    for i in range(1, part_ref.shape[0]):
        packed = packed + part_ref[i]
    size = RUNS * STEPS
    raw = jnp.concatenate(
        [packed if j == 0 else pltpu.roll(packed, 128 - size * j, 1) for j in range(STEPS)], axis=0
    )
    sub = sub_iota((size, 128))
    lane = lane_iota((size, 128))
    raw = jnp.where(lane < size, raw, 0.0)
    square = jnp.concatenate([raw, jnp.zeros((128 - size, 128), jnp.float32)], axis=0)
    mirror = square.T[:size, :]
    raw = jnp.where((sub >> 3) <= (lane >> 3), raw, mirror)
    source = 8 * (sub & 3) + (sub >> 2)
    perm = jnp.where(lane == source, 1.0, 0.0)
    rows = dot(perm[:, :size], raw)
    target = 8 * (lane & 3) + (lane >> 2)
    perm_t = jnp.where((sub == target) & (lane < size), 1.0, 0.0)
    full = dot(rows[:, :size], perm_t)
    diag = jnp.where(sub == lane, full, 0.0)
    mu_col = jnp.sum(diag, axis=1, keepdims=True) / CELLS
    mu_row = jnp.sum(diag, axis=0, keepdims=True) / CELLS
    scale_col = 1.0 / jnp.sqrt(mu_col + EPS)
    scale_row = 1.0 / jnp.sqrt(mu_row + EPS)
    gram_now = full * scale_col * scale_row / CELLS
    nodes = RUNS // 2
    first_node = 0
    total = None
    while nodes:
        basis = level_basis(gram_now, nodes, first_node, order_ref, keep_ref)
        w = weights(basis, nodes)
        rows_now = 8 * nodes
        total = w if total is None else dot(total[:, :rows_now], w)
        if nodes > 1:
            half = dot(gram_now[:, :rows_now], w)
            w_t = jnp.concatenate([w, jnp.zeros((128 - rows_now, 128), jnp.float32)], axis=0).T
            gram_now = dot(w_t[: STEPS * nodes, :rows_now], half)
        first_node += nodes
        nodes //= 2
    total = total * scale_col
    for c in range(STEPS):
        w_ref[c] = jnp.broadcast_to(total[:, c : c + 1], (size, 128))
    for l in range(NZ // 128):
        cols = slice(128 * l, 128 * l + 128)
        for i in range(BLOCK // 8):
            rws = slice(8 * i, 8 * i + 8)
            accs = [None] * STEPS
            for q in range(RUNS):
                for t in range(STEPS):
                    x = cores[t][q][rws, cols]
                    k = STEPS * q + t
                    for c in range(STEPS):
                        term = w_ref[c, k : k + 1, :] * x
                        accs[c] = term if accs[c] is None else accs[c] + term
            for c in range(STEPS):
                out_ref[c, 0, rws, cols] = accs[c]


def finish(order, keep, parts, cores):
    return pl.pallas_call(
        finish_kernel,
        out_shape=jax.ShapeDtypeStruct((STEPS, 1, BLOCK, NZ), jnp.float32),
        in_specs=[SMEM, SMEM, VMEM] + [VMEM] * (STEPS * len(GROUPS)),
        out_specs=VMEM,
        scratch_shapes=[pltpu.VMEM((STEPS, RUNS * STEPS, 128), jnp.float32)],
        compiler_params=params(),
        cost_estimate=pl.CostEstimate(flops=5000000, bytes_accessed=2400000, transcendentals=0),
        name="finish",
    )(order, keep, parts, *[piece for core in cores for piece in core])


def local(start_field, viscosity, diffusivity, velocity, assignment, child_order, keep_ranks):
    coefs = (diffusivity, velocity, assignment)
    sibling = [(i, i ^ 1) for i in range(NX)]
    crossing = [(i, i + 1) for i in range(1, NX - 1, 2)] + [(i + 1, i) for i in range(1, NX - 1, 2)]
    blocks, visc = row_blocks(start_field, viscosity)
    states = list(assemble(lax.all_to_all(blocks, "run", 0, 0), visc))
    cores = []
    packed = None
    for step in range(STEPS):
        last = step == STEPS - 1
        halos = []
        for state in states:
            sib = lax.ppermute(state, SPACE, sibling)
            cross = lax.ppermute(state, SPACE, crossing)
            halos.append((sib, cross))
        if step == 0:
            around = halos[0]
        if cores:
            packed = gram(cores, packed, False)
        results = [
            advance(last, group, coefs, state, *halo, visc, *around)
            for group, state, halo in zip(GROUPS, states, halos)
        ]
        cores.append([result[-1] for result in results])
        states = [result[0] for result in results]
    parts = gram(cores, packed, True)
    parts = spread(lax.all_to_all(parts, ("y", "core"), 0, 0))
    parts = lax.all_to_all(parts, ("run", "x"), 0, 0)
    return finish(child_order, keep_ranks, parts, cores)


def solution(mesh):
    fine = Mesh(mesh.devices.reshape(8, 4, 8, 2), ("run", "x", "y", "core"))
    in_specs = (P("run", SPACE, None, None), P(SPACE, None, None), P(), P(), P(), P(), P())
    out_specs = P(None, SPACE, "run", None)
    return jax.shard_map(local, mesh=fine, in_specs=in_specs, out_specs=out_specs, check_vma=False)
```

```python
import math

import jax
import jax.numpy as jnp
from jax import lax
from jax.experimental import pallas as pl
from jax.experimental.pallas import tpu as pltpu
from jax.sharding import Mesh, PartitionSpec as P

STEPS = 4
SUBITERS = 3
EPS = 1e-06
RUNS = 8
NY = 256
NZ = 512
NX = 64
BLOCK = NY // RUNS
HALO = STEPS
EXT = BLOCK + 2 * HALO
CELLS = NX * NY * NZ
EXACT = lax.Precision.HIGHEST
SPACE = ("x", "y", "core")
FIRST = 16
SECOND = 32
VMEM = pl.BlockSpec(memory_space=pltpu.VMEM)
SMEM = pl.BlockSpec(memory_space=pltpu.SMEM)


def sub_iota(shape):
    return lax.broadcasted_iota(jnp.int32, shape, 0)


def lane_iota(shape):
    return lax.broadcasted_iota(jnp.int32, shape, 1)


def params(limit=40 << 20):
    return pltpu.CompilerParams(vmem_limit_bytes=limit)


ROWS = 8
TILES = NY // 8


def shifted(before, after):
    low = sub_iota((8, NZ)) < 4
    return pltpu.roll(jnp.where(low, after, before), 4, 0)


def blocks_kernel(field_ref, out_ref):
    zero = jnp.zeros((8, NZ), jnp.float32)
    before = zero
    for m in range(TILES + 1):
        after = field_ref[0, 0, 8 * m : 8 * m + 8, :] if m < TILES else zero
        tile = shifted(before, after)
        before = after
        for q in range(RUNS):
            j = m - 4 * q
            if 0 <= j <= 4:
                out_ref[q, 8 * j : 8 * j + 8, :] = tile


def row_blocks(field):
    return pl.pallas_call(
        blocks_kernel,
        out_shape=jax.ShapeDtypeStruct((RUNS, EXT, NZ), jnp.float32),
        in_specs=[VMEM],
        out_specs=VMEM,
        compiler_params=params(),
        cost_estimate=pl.CostEstimate(flops=200000, bytes_accessed=1200000, transcendentals=0),
        name="row_blocks",
    )(field)


def rates_kernel(diff_ref, vel_ref, assign_ref, table_ref):
    even = lax.axis_index("core") == 0
    for q in range(RUNS):
        s = assign_ref[q]
        ups = [-jnp.minimum(vel_ref[d, s], 0.0) for d in range(3)]
        downs = [jnp.maximum(vel_ref[d, s], 0.0) for d in range(3)]
        w_sib = jnp.where(even, ups[0], downs[0])
        w_cross = jnp.where(even, downs[0], ups[0])
        values = (0.5 * diff_ref[s], w_sib, w_cross, ups[1], downs[1], ups[2], downs[2])
        for k, value in enumerate(values):
            table_ref[ROWS * q + k : ROWS * q + k + 1, :] = jnp.full((1, NZ), value, jnp.float32)


def run_rates(diffusivity, velocity, assignment):
    return pl.pallas_call(
        rates_kernel,
        out_shape=jax.ShapeDtypeStruct((ROWS * RUNS, NZ), jnp.float32),
        in_specs=[SMEM, SMEM, SMEM],
        out_specs=VMEM,
        compiler_params=params(),
        cost_estimate=pl.CostEstimate(flops=0, bytes_accessed=140000, transcendentals=0),
        name="rates",
    )(diffusivity, velocity.T, assignment)


def assemble_kernel(state_ref, visc_ref, out_ref):
    run = lax.axis_index("run")
    for q in range(RUNS):
        out_ref[q] = state_ref[q]
    for j in range(5):
        m = 4 * run + j
        prev_at = pl.multiple_of(8 * jnp.maximum(m - 1, 0), 8)
        next_at = pl.multiple_of(8 * jnp.minimum(m, TILES - 1), 8)
        prev = jnp.where(m > 0, visc_ref[0, pl.ds(prev_at, 8), :], 0.0)
        nxt = jnp.where(m < TILES, visc_ref[0, pl.ds(next_at, 8), :], 0.0)
        out_ref[RUNS, 8 * j : 8 * j + 8, :] = shifted(prev, nxt)


def assemble(state, visc):
    return pl.pallas_call(
        assemble_kernel,
        out_shape=jax.ShapeDtypeStruct((RUNS + 1, EXT, NZ), jnp.float32),
        in_specs=[VMEM, VMEM],
        out_specs=VMEM,
        compiler_params=params(),
        cost_estimate=pl.CostEstimate(flops=0, bytes_accessed=1400000, transcendentals=0),
        name="assemble",
    )(state, visc)


def interior_kernel(u_ref, v_ref, table_ref, out_ref):
    col = lane_iota((EXT, NZ))
    first_col = col == 0
    last_col = col == NZ - 1
    v = v_ref[RUNS]

    def ahead_row(a):
        return pltpu.roll(a, EXT - 1, 0)

    def behind_row(a):
        return pltpu.roll(a, 1, 0)

    def ahead_col(a):
        return jnp.where(last_col, 0.0, pltpu.roll(a, NZ - 1, 1))

    def behind_col(a):
        return jnp.where(first_col, 0.0, pltpu.roll(a, 1, 1))

    moves = (ahead_row, behind_row, ahead_col, behind_col)
    coefs = [v + move(v) for move in moves]
    for q in range(RUNS):
        u = u_ref[q]
        rates = [table_ref[ROWS * q + k : ROWS * q + k + 1, :] for k in range(7)]
        new = u
        for k, move in enumerate(moves):
            new = new + (rates[0] * coefs[k] + rates[3 + k]) * (move(u) - u)
        out_ref[q] = new


def interior(state, visc, table):
    return pl.pallas_call(
        interior_kernel,
        out_shape=jax.ShapeDtypeStruct((RUNS, EXT, NZ), jnp.float32),
        in_specs=[VMEM] * 3,
        out_specs=VMEM,
        compiler_params=params(),
        cost_estimate=pl.CostEstimate(flops=4000000, bytes_accessed=1400000, transcendentals=0),
        name="interior",
    )(state, visc, table)


def close_kernel(edge, want, acc_ref, u_ref, sib_ref, cross_ref, v_ref, vs_ref, vc_ref, table_ref, *outs):
    run = lax.axis_index("run")
    row = sub_iota((EXT, NZ)) + (BLOCK * run - HALO)
    inside = (row >= 0) & (row < NY)
    if edge:
        place = (lax.axis_index("x") * 8 + lax.axis_index("y")) * 2 + lax.axis_index("core")
        inside = inside & (place > 0) & (place < NX - 1)
    v = v_ref[RUNS]
    c_sib = v + vs_ref[RUNS]
    c_cross = v + vc_ref[RUNS]
    for q in range(RUNS):
        rates = [table_ref[ROWS * q + k : ROWS * q + k + 1, :] for k in range(3)]
        u = u_ref[q]
        new = acc_ref[q] + (rates[0] * c_sib + rates[1]) * (sib_ref[q] - u)
        new = new + (rates[0] * c_cross + rates[2]) * (cross_ref[q] - u)
        new = jnp.where(inside, new, 0.0)
        if "full" in want:
            outs[0][q] = new
        if "core" in want:
            outs[-1][q] = pltpu.roll(new, EXT - HALO, 0)[:BLOCK]


def close(want, acc, u, sib, cross, v, v_sib, v_cross, table, edge=False):
    sizes = [EXT] * ("full" in want) + [BLOCK] * ("core" in want)
    args = [acc, u, sib, cross, v, v_sib, v_cross, table]

    def body(*refs):
        close_kernel(edge, want, *refs)

    return pl.pallas_call(
        body,
        out_shape=tuple(jax.ShapeDtypeStruct((RUNS, rows, NZ), jnp.float32) for rows in sizes),
        in_specs=[VMEM] * len(args),
        out_specs=tuple(VMEM for _ in sizes),
        compiler_params=params(),
        cost_estimate=pl.CostEstimate(flops=1200000, bytes_accessed=1600000, transcendentals=0),
        name="close_" + "_".join(want),
    )(*args)


def merge(x, y, width):
    sub = sub_iota((8, 128))
    pick = (sub & width) == 0
    keep = jnp.where(pick, x, y)
    give = jnp.where(pick, y, x)
    if width == 4:
        moved = pltpu.roll(give, 4, 0)
    else:
        moved = jnp.where(pick, pltpu.roll(give, 8 - width, 0), pltpu.roll(give, width, 0))
    return keep + moved


def gram_kernel(group, last, *refs):
    cores = refs[: group + 1]
    prev_ref = refs[group + 1] if group else None
    out_ref = refs[-1]
    mine = cores[group]
    lane = lane_iota((8, 128))
    packed = prev_ref[...] if group else jnp.zeros((8, 128), jnp.float32)
    for other in range(group + 1):
        theirs = cores[other]
        for half in range(2):
            first = 4 if other == group and half else 0
            wide = 8 - first
            accs = tuple(jnp.zeros((8, 128), jnp.float32) for _ in range(4 * wide))

            def body(i, accs, theirs=theirs, half=half, first=first, wide=wide):
                rows = pl.ds(pl.multiple_of(8 * i, 8), 8)
                accs = list(accs)
                for l in range(NZ // 128):
                    cols = slice(128 * l, 128 * l + 128)
                    a = [mine[4 * half + k, rows, cols] for k in range(4)]
                    for b in range(wide):
                        t = theirs[first + b, rows, cols]
                        for k in range(4):
                            accs[wide * k + b] = accs[wide * k + b] + a[k] * t
                return tuple(accs)

            accs = lax.fori_loop(0, BLOCK // 8, body, accs)
            for k in range(4):
                level = [jnp.zeros((8, 128), jnp.float32)] * first + list(accs[wide * k : wide * k + wide])
                for width in (4, 2, 1):
                    count = len(level) // 2
                    level = [merge(level[i], level[i + count], width) for i in range(count)]
                total = jnp.sum(level[0], axis=1, keepdims=True)
                at = 32 * other + STEPS * (4 * half + k) + group
                packed = jnp.where(lane == at, total, packed)
    if last:
        for i in range(FIRST):
            out_ref[i] = packed
    else:
        out_ref[...] = packed


def gram(cores, prev, last):
    group = len(cores) - 1
    shape = (FIRST, 8, 128) if last else (8, 128)
    args = list(cores) + ([prev] if group else [])

    def body(*refs):
        gram_kernel(group, last, *refs)

    return pl.pallas_call(
        body,
        out_shape=jax.ShapeDtypeStruct(shape, jnp.float32),
        in_specs=[VMEM] * len(args),
        out_specs=VMEM,
        compiler_params=params(),
        cost_estimate=pl.CostEstimate(flops=2200000 * (group + 1), bytes_accessed=600000 * (group + 1), transcendentals=0),
        name=f"gram{group}",
    )(*args)


def spread_kernel(in_ref, out_ref):
    total = in_ref[0]
    for i in range(1, FIRST):
        total = total + in_ref[i]
    for i in range(SECOND):
        out_ref[i] = total


def spread(parts):
    return pl.pallas_call(
        spread_kernel,
        out_shape=jax.ShapeDtypeStruct((SECOND, 8, 128), jnp.float32),
        in_specs=[VMEM],
        out_specs=VMEM,
        compiler_params=params(),
        name="spread",
    )(parts)


def dot(a, b):
    return jnp.dot(a, b, precision=EXACT, preferred_element_type=jnp.float32)


def dct():
    size = 2 * STEPS
    return [
        [math.sqrt(1.0 / STEPS) * math.cos(math.pi * (i + 0.5) * (j + 0.5) / size) for j in range(STEPS)]
        for i in range(size)
    ]


def sublane_sum(a):
    for width in (4, 2, 1):
        a = a + pltpu.roll(a, width, 0)
    return a


def level_basis(gram_now, nodes, first_node, order_ref, keep_ref):
    shape = (8, 128)
    sub = sub_iota(shape)
    lane = lane_iota(shape) & (nodes - 1)
    table = dct()
    basis = [jnp.zeros(shape, jnp.float32) for _ in range(STEPS)]
    live = [jnp.zeros(shape, jnp.float32) for _ in range(STEPS)]
    for k in range(nodes):
        node = first_node + k
        here = lane == k
        for c in range(STEPS):
            flag = jnp.where(keep_ref[node] > c, 1.0, 0.0)
            live[c] = jnp.where(here, flag, live[c])
        for i in range(2 * STEPS):
            spot = here & (sub == order_ref[node, i])
            for c in range(STEPS):
                basis[c] = jnp.where(spot, table[i][c], basis[c])
    basis = [z * m for z, m in zip(basis, live)]
    cols = []
    for j in range(8):
        col = jnp.zeros(shape, jnp.float32)
        for k in range(nodes):
            piece = gram_now[8 * k : 8 * k + 8, 8 * k + j : 8 * k + j + 1]
            col = jnp.where(lane == k, piece, col)
        cols.append(col)
    for _ in range(SUBITERS):
        image = []
        for c in range(STEPS):
            total = cols[0] * basis[c][0:1, :]
            for j in range(1, 8):
                total = total + cols[j] * basis[c][j : j + 1, :]
            image.append(total * live[c])
        inner = {}
        for a in range(STEPS):
            for b in range(a + 1):
                inner[a, b] = sublane_sum(image[a] * image[b])
            inner[a, a] = inner[a, a] + (1.0 - live[a])
        low = {}
        inv = []
        for b in range(STEPS):
            pivot = inner[b, b]
            for k in range(b):
                pivot = pivot - low[b, k] * low[b, k]
            root = 1.0 / jnp.sqrt(pivot)
            inv.append(root)
            for a in range(b + 1, STEPS):
                entry = inner[a, b]
                for k in range(b):
                    entry = entry - low[a, k] * low[b, k]
                low[a, b] = entry * root
        fresh = []
        for a in range(STEPS):
            value = image[a]
            for k in range(a):
                value = value - low[a, k] * fresh[k]
            fresh.append(value * inv[a])
        basis = fresh
    return basis


def weights(basis, nodes):
    lane = lane_iota((8, 128))
    rows = []
    for k in range(nodes):
        block = jnp.zeros((8, 128), jnp.float32)
        for c in range(STEPS):
            block = jnp.where(lane == STEPS * k + c, basis[c][:, k : k + 1], block)
        rows.append(block)
    return jnp.concatenate(rows, axis=0) if nodes > 1 else rows[0]


def finish_kernel(order_ref, keep_ref, part_ref, *refs):
    out_ref, w_ref = refs[-2:]
    cores = refs[:STEPS]
    packed = part_ref[0]
    for i in range(1, part_ref.shape[0]):
        packed = packed + part_ref[i]
    size = RUNS * STEPS
    raw = jnp.concatenate(
        [packed if j == 0 else pltpu.roll(packed, 128 - size * j, 1) for j in range(STEPS)], axis=0
    )
    sub = sub_iota((size, 128))
    lane = lane_iota((size, 128))
    raw = jnp.where(lane < size, raw, 0.0)
    perm = jnp.where(lane == 8 * (sub & 3) + (sub >> 2), 1.0, 0.0)
    full = dot(perm[:, :size], raw)
    square = jnp.concatenate([full, jnp.zeros((128 - size, 128), jnp.float32)], axis=0)
    mirror = square.T[:size, :]
    same = ((sub & 3) == (lane & 3)) & (((lane & 16) == 0) | ((sub & 16) != 0))
    full = jnp.where(((sub & 3) < (lane & 3)) | same, full, mirror)
    diag = jnp.where(sub == lane, full, 0.0)
    mu_col = jnp.sum(diag, axis=1, keepdims=True) / CELLS
    mu_row = jnp.sum(diag, axis=0, keepdims=True) / CELLS
    scale_col = 1.0 / jnp.sqrt(mu_col + EPS)
    scale_row = 1.0 / jnp.sqrt(mu_row + EPS)
    gram_now = full * scale_col * scale_row / CELLS
    nodes = RUNS // 2
    first_node = 0
    total = None
    while nodes:
        basis = level_basis(gram_now, nodes, first_node, order_ref, keep_ref)
        w = weights(basis, nodes)
        rows_now = 8 * nodes
        total = w if total is None else dot(total[:, :rows_now], w)
        if nodes > 1:
            half = dot(gram_now[:, :rows_now], w)
            w_t = jnp.concatenate([w, jnp.zeros((128 - rows_now, 128), jnp.float32)], axis=0).T
            gram_now = dot(w_t[: STEPS * nodes, :rows_now], half)
        first_node += nodes
        nodes //= 2
    total = total * scale_col
    for c in range(STEPS):
        w_ref[c] = jnp.broadcast_to(total[:, c : c + 1], (size, 128))
    for l in range(NZ // 128):
        cols = slice(128 * l, 128 * l + 128)
        for i in range(BLOCK // 8):
            rws = slice(8 * i, 8 * i + 8)
            accs = [None] * STEPS
            for q in range(RUNS):
                for t in range(STEPS):
                    x = cores[t][q, rws, cols]
                    k = STEPS * q + t
                    for c in range(STEPS):
                        term = w_ref[c, k : k + 1, :] * x
                        accs[c] = term if accs[c] is None else accs[c] + term
            for c in range(STEPS):
                out_ref[c, 0, rws, cols] = accs[c]


def finish(order, keep, parts, cores):
    return pl.pallas_call(
        finish_kernel,
        out_shape=jax.ShapeDtypeStruct((STEPS, 1, BLOCK, NZ), jnp.float32),
        in_specs=[SMEM, SMEM, VMEM] + [VMEM] * STEPS,
        out_specs=VMEM,
        scratch_shapes=[pltpu.VMEM((STEPS, RUNS * STEPS, 128), jnp.float32)],
        compiler_params=params(),
        cost_estimate=pl.CostEstimate(flops=5000000, bytes_accessed=2400000, transcendentals=0),
        name="finish",
    )(order, keep, parts, *cores)


def local(start_field, viscosity, diffusivity, velocity, assignment, child_order, keep_ranks):
    sibling = [(i, i ^ 1) for i in range(NX)]
    crossing = [(i, i + 1) for i in range(1, NX - 1, 2)] + [(i + 1, i) for i in range(1, NX - 1, 2)]
    blocks = lax.all_to_all(row_blocks(start_field), "run", 0, 0)
    own = assemble(blocks, viscosity)
    table = run_rates(diffusivity, velocity, assignment)
    planes = None
    cores = []
    packed = None

    def swap_cross(a):
        return lax.ppermute(a, SPACE, crossing)

    def swap_sib(a):
        return lax.ppermute(a, SPACE, sibling)

    for turn in range(STEPS // 2):
        sib1 = swap_sib(own)
        cross1 = swap_cross(own)
        if planes is None:
            v, vs1, vc1 = own, sib1, cross1
        acc_own = interior(own, v, table)
        acc_sib = interior(sib1, vs1, table)
        last = turn == STEPS // 2 - 1
        cross2 = swap_cross(sib1)
        sib2 = swap_sib(cross1)
        if planes is None:
            planes = vs2, vc2 = sib2, cross2
        acc_cross = interior(cross1, vc1, table)
        fresh, core = close(("full", "core"), acc_own, own, sib1, cross1, v, vs1, vc1, table)
        cores.append(core)
        packed = gram(cores, packed, False)
        (near_sib,) = close(("full",), acc_sib, sib1, sib2, own, vs1, vs2, v, table)
        acc_own = interior(fresh, v, table)
        (near_cross,) = close(("full",), acc_cross, cross1, own, cross2, vc1, v, vc2, table, edge=True)
        want = ("core",) if last else ("full", "core")
        result = close(want, acc_own, fresh, near_sib, near_cross, v, vs1, vc1, table)
        cores.append(result[-1])
        own = result[0]
        if not last:
            packed = gram(cores, packed, False)
    parts = gram(cores, packed, True)
    parts = spread(lax.all_to_all(parts, ("y", "core"), 0, 0))
    parts = lax.all_to_all(parts, ("run", "x"), 0, 0)
    return finish(child_order, keep_ranks, parts, cores)


def solution(mesh):
    fine = Mesh(mesh.devices.reshape(8, 4, 8, 2), ("run", "x", "y", "core"))
    in_specs = (P("run", SPACE, None, None), P(SPACE, None, None), P(), P(), P(), P(), P())
    out_specs = P(None, SPACE, "run", None)
    return jax.shard_map(local, mesh=fine, in_specs=in_specs, out_specs=out_specs, check_vma=False)
```

```python
import math

import jax
import jax.numpy as jnp
from jax import lax
from jax.experimental import pallas as pl
from jax.experimental.pallas import tpu as pltpu
from jax.sharding import Mesh, PartitionSpec as P

STEPS = 4
SUBITERS = 3
EPS = 1e-06
RUNS = 8
NY = 256
NZ = 512
NX = 64
BLOCK = NY // RUNS
HALO = STEPS
EXT = BLOCK + 2 * HALO
CELLS = NX * NY * NZ
EXACT = lax.Precision.HIGHEST
SPACE = ("x", "y", "core")
FIRST = 16
SECOND = 32
VMEM = pl.BlockSpec(memory_space=pltpu.VMEM)
SMEM = pl.BlockSpec(memory_space=pltpu.SMEM)


def sub_iota(shape):
    return lax.broadcasted_iota(jnp.int32, shape, 0)


def lane_iota(shape):
    return lax.broadcasted_iota(jnp.int32, shape, 1)


def params(limit=40 << 20):
    return pltpu.CompilerParams(vmem_limit_bytes=limit)


ROWS = 8
TILES = NY // 8


def shifted(before, after):
    low = sub_iota((8, NZ)) < 4
    return pltpu.roll(jnp.where(low, after, before), 4, 0)


def blocks_kernel(field_ref, out_ref):
    zero = jnp.zeros((8, NZ), jnp.float32)
    before = zero
    for m in range(TILES + 1):
        after = field_ref[0, 0, 8 * m : 8 * m + 8, :] if m < TILES else zero
        tile = shifted(before, after)
        before = after
        for q in range(RUNS):
            j = m - 4 * q
            if 0 <= j <= 4:
                out_ref[q, 8 * j : 8 * j + 8, :] = tile


def row_blocks(field):
    return pl.pallas_call(
        blocks_kernel,
        out_shape=jax.ShapeDtypeStruct((RUNS, EXT, NZ), jnp.float32),
        in_specs=[VMEM],
        out_specs=VMEM,
        compiler_params=params(),
        cost_estimate=pl.CostEstimate(flops=200000, bytes_accessed=1200000, transcendentals=0),
        name="row_blocks",
    )(field)


def rates_kernel(diff_ref, vel_ref, assign_ref, table_ref):
    even = lax.axis_index("core") == 0
    for q in range(RUNS):
        s = assign_ref[q]
        ups = [-jnp.minimum(vel_ref[d, s], 0.0) for d in range(3)]
        downs = [jnp.maximum(vel_ref[d, s], 0.0) for d in range(3)]
        w_sib = jnp.where(even, ups[0], downs[0])
        w_cross = jnp.where(even, downs[0], ups[0])
        values = (0.5 * diff_ref[s], w_sib, w_cross, ups[1], downs[1], ups[2], downs[2])
        for k, value in enumerate(values):
            table_ref[ROWS * q + k : ROWS * q + k + 1, :] = jnp.full((1, NZ), value, jnp.float32)


def run_rates(diffusivity, velocity, assignment):
    return pl.pallas_call(
        rates_kernel,
        out_shape=jax.ShapeDtypeStruct((ROWS * RUNS, NZ), jnp.float32),
        in_specs=[SMEM, SMEM, SMEM],
        out_specs=VMEM,
        compiler_params=params(),
        cost_estimate=pl.CostEstimate(flops=0, bytes_accessed=140000, transcendentals=0),
        name="rates",
    )(diffusivity, velocity.T, assignment)


def assemble_kernel(state_ref, visc_ref, out_ref):
    run = lax.axis_index("run")
    for q in range(RUNS):
        out_ref[q] = state_ref[q]
    for j in range(5):
        m = 4 * run + j
        prev_at = pl.multiple_of(8 * jnp.maximum(m - 1, 0), 8)
        next_at = pl.multiple_of(8 * jnp.minimum(m, TILES - 1), 8)
        prev = jnp.where(m > 0, visc_ref[0, pl.ds(prev_at, 8), :], 0.0)
        nxt = jnp.where(m < TILES, visc_ref[0, pl.ds(next_at, 8), :], 0.0)
        out_ref[RUNS, 8 * j : 8 * j + 8, :] = shifted(prev, nxt)


def assemble(state, visc):
    return pl.pallas_call(
        assemble_kernel,
        out_shape=jax.ShapeDtypeStruct((RUNS + 1, EXT, NZ), jnp.float32),
        in_specs=[VMEM, VMEM],
        out_specs=VMEM,
        compiler_params=params(),
        cost_estimate=pl.CostEstimate(flops=0, bytes_accessed=1400000, transcendentals=0),
        name="assemble",
    )(state, visc)


def trim_kernel(in_ref, out_ref):
    for q in range(RUNS):
        out_ref[q] = pltpu.roll(in_ref[q], EXT - HALO, 0)[:BLOCK]


def trim(plane):
    return pl.pallas_call(
        trim_kernel,
        out_shape=jax.ShapeDtypeStruct((RUNS, BLOCK, NZ), jnp.float32),
        in_specs=[VMEM],
        out_specs=VMEM,
        compiler_params=params(),
        cost_estimate=pl.CostEstimate(flops=0, bytes_accessed=1200000, transcendentals=0),
        name="trim",
    )(plane)


def interior_kernel(u_ref, v_ref, table_ref, out_ref):
    col = lane_iota((EXT, NZ))
    first_col = col == 0
    last_col = col == NZ - 1
    v = v_ref[RUNS]

    def ahead_row(a):
        return pltpu.roll(a, EXT - 1, 0)

    def behind_row(a):
        return pltpu.roll(a, 1, 0)

    def ahead_col(a):
        return jnp.where(last_col, 0.0, pltpu.roll(a, NZ - 1, 1))

    def behind_col(a):
        return jnp.where(first_col, 0.0, pltpu.roll(a, 1, 1))

    moves = (ahead_row, behind_row, ahead_col, behind_col)
    coefs = [v + move(v) for move in moves]
    for q in range(RUNS):
        u = u_ref[q]
        rates = [table_ref[ROWS * q + k : ROWS * q + k + 1, :] for k in range(7)]
        new = u
        for k, move in enumerate(moves):
            new = new + (rates[0] * coefs[k] + rates[3 + k]) * (move(u) - u)
        out_ref[q] = new


def interior(state, visc, table):
    return pl.pallas_call(
        interior_kernel,
        out_shape=jax.ShapeDtypeStruct((RUNS, EXT, NZ), jnp.float32),
        in_specs=[VMEM] * 3,
        out_specs=VMEM,
        compiler_params=params(),
        cost_estimate=pl.CostEstimate(flops=4000000, bytes_accessed=1400000, transcendentals=0),
        name="interior",
    )(state, visc, table)


def padded(rows):
    if rows.shape[0] == EXT:
        return rows
    return pltpu.roll(jnp.concatenate([rows, jnp.zeros((2 * HALO, NZ), jnp.float32)], axis=0), HALO, 0)


def close_kernel(edge, want, acc_ref, u_ref, sib_ref, cross_ref, v_ref, vs_ref, vc_ref, table_ref, *outs):
    run = lax.axis_index("run")
    row = sub_iota((EXT, NZ)) + (BLOCK * run - HALO)
    inside = (row >= 0) & (row < NY)
    if edge:
        place = (lax.axis_index("x") * 8 + lax.axis_index("y")) * 2 + lax.axis_index("core")
        inside = inside & (place > 0) & (place < NX - 1)
    v = v_ref[RUNS]
    c_sib = v + vs_ref[RUNS]
    c_cross = v + vc_ref[RUNS]
    for q in range(RUNS):
        rates = [table_ref[ROWS * q + k : ROWS * q + k + 1, :] for k in range(3)]
        u = u_ref[q]
        new = acc_ref[q] + (rates[0] * c_sib + rates[1]) * (padded(sib_ref[q]) - u)
        across = padded(cross_ref[q])
        new = new + (rates[0] * c_cross + rates[2]) * (across - u)
        new = jnp.where(inside, new, 0.0)
        if "full" in want:
            outs[0][q] = new
        if "core" in want:
            outs[-1][q] = pltpu.roll(new, EXT - HALO, 0)[:BLOCK]


def close(want, acc, u, sib, cross, v, v_sib, v_cross, table, edge=False):
    sizes = [EXT] * ("full" in want) + [BLOCK] * ("core" in want)
    args = [acc, u, sib, cross, v, v_sib, v_cross, table]

    def body(*refs):
        close_kernel(edge, want, *refs)

    return pl.pallas_call(
        body,
        out_shape=tuple(jax.ShapeDtypeStruct((RUNS, rows, NZ), jnp.float32) for rows in sizes),
        in_specs=[VMEM] * len(args),
        out_specs=tuple(VMEM for _ in sizes),
        compiler_params=params(),
        cost_estimate=pl.CostEstimate(flops=1200000, bytes_accessed=1600000, transcendentals=0),
        name="close_" + "_".join(want),
    )(*args)


def merge(x, y, width):
    sub = sub_iota((8, 128))
    pick = (sub & width) == 0
    keep = jnp.where(pick, x, y)
    give = jnp.where(pick, y, x)
    if width == 4:
        moved = pltpu.roll(give, 4, 0)
    else:
        moved = jnp.where(pick, pltpu.roll(give, 8 - width, 0), pltpu.roll(give, width, 0))
    return keep + moved


def gram_kernel(group, last, *refs):
    cores = refs[: group + 1]
    prev_ref = refs[group + 1] if group else None
    out_ref = refs[-1]
    mine = cores[group]
    lane = lane_iota((8, 128))
    packed = prev_ref[...] if group else jnp.zeros((8, 128), jnp.float32)
    for other in range(group + 1):
        theirs = cores[other]
        for half in range(2):
            first = 4 if other == group and half else 0
            wide = 8 - first
            accs = tuple(jnp.zeros((8, 128), jnp.float32) for _ in range(4 * wide))

            def body(i, accs, theirs=theirs, half=half, first=first, wide=wide):
                rows = slice(8 * i, 8 * i + 8)
                accs = list(accs)
                for l in range(NZ // 128):
                    cols = slice(128 * l, 128 * l + 128)
                    a = [mine[4 * half + k, rows, cols] for k in range(4)]
                    for b in range(wide):
                        t = theirs[first + b, rows, cols]
                        for k in range(4):
                            accs[wide * k + b] = accs[wide * k + b] + a[k] * t
                return tuple(accs)

            for i in range(BLOCK // 8):
                accs = body(i, accs)
            for k in range(4):
                level = [jnp.zeros((8, 128), jnp.float32)] * first + list(accs[wide * k : wide * k + wide])
                for width in (4, 2, 1):
                    count = len(level) // 2
                    level = [merge(level[i], level[i + count], width) for i in range(count)]
                total = jnp.sum(level[0], axis=1, keepdims=True)
                at = 32 * other + STEPS * (4 * half + k) + group
                packed = jnp.where(lane == at, total, packed)
    if last:
        for i in range(FIRST):
            out_ref[i] = packed
    else:
        out_ref[...] = packed


def gram(cores, prev, last):
    group = len(cores) - 1
    shape = (FIRST, 8, 128) if last else (8, 128)
    args = list(cores) + ([prev] if group else [])

    def body(*refs):
        gram_kernel(group, last, *refs)

    return pl.pallas_call(
        body,
        out_shape=jax.ShapeDtypeStruct(shape, jnp.float32),
        in_specs=[VMEM] * len(args),
        out_specs=VMEM,
        compiler_params=params(),
        cost_estimate=pl.CostEstimate(flops=2200000 * (group + 1), bytes_accessed=600000 * (group + 1), transcendentals=0),
        name=f"gram{group}",
    )(*args)


def spread_kernel(in_ref, out_ref):
    total = in_ref[0]
    for i in range(1, FIRST):
        total = total + in_ref[i]
    for i in range(SECOND):
        out_ref[i] = total


def spread(parts):
    return pl.pallas_call(
        spread_kernel,
        out_shape=jax.ShapeDtypeStruct((SECOND, 8, 128), jnp.float32),
        in_specs=[VMEM],
        out_specs=VMEM,
        compiler_params=params(),
        name="spread",
    )(parts)


def dot(a, b):
    return jnp.dot(a, b, precision=EXACT, preferred_element_type=jnp.float32)


def dct():
    size = 2 * STEPS
    return [
        [math.sqrt(1.0 / STEPS) * math.cos(math.pi * (i + 0.5) * (j + 0.5) / size) for j in range(STEPS)]
        for i in range(size)
    ]


def sublane_sum(a):
    for width in (4, 2, 1):
        a = a + pltpu.roll(a, width, 0)
    return a


def starts_kernel(order_ref, keep_ref, out_ref):
    shape = (8, 128)
    sub = sub_iota(shape)
    table = dct()
    nodes = RUNS // 2
    first_node = 0
    level = 0
    while nodes:
        lane = lane_iota(shape) & (nodes - 1)
        basis = [jnp.zeros(shape, jnp.float32) for _ in range(STEPS)]
        live = [jnp.zeros(shape, jnp.float32) for _ in range(STEPS)]
        for k in range(nodes):
            node = first_node + k
            here = lane == k
            for c in range(STEPS):
                flag = jnp.where(keep_ref[node] > c, 1.0, 0.0)
                live[c] = jnp.where(here, flag, live[c])
            for i in range(2 * STEPS):
                spot = here & (sub == order_ref[node, i])
                for c in range(STEPS):
                    basis[c] = jnp.where(spot, table[i][c], basis[c])
        for c in range(STEPS):
            out_ref[2 * STEPS * level + c] = basis[c] * live[c]
            out_ref[2 * STEPS * level + STEPS + c] = live[c]
        first_node += nodes
        nodes //= 2
        level += 1


def starts(order, keep):
    return pl.pallas_call(
        starts_kernel,
        out_shape=jax.ShapeDtypeStruct((3 * 2 * STEPS, 8, 128), jnp.float32),
        in_specs=[SMEM, SMEM],
        out_specs=VMEM,
        compiler_params=params(),
        cost_estimate=pl.CostEstimate(flops=0, bytes_accessed=100000, transcendentals=0),
        name="starts",
    )(order, keep)


def level_basis(gram_now, nodes, level, start_ref):
    shape = (8, 128)
    lane = lane_iota(shape) & (nodes - 1)
    basis = [start_ref[2 * STEPS * level + c] for c in range(STEPS)]
    live = [start_ref[2 * STEPS * level + STEPS + c] for c in range(STEPS)]
    cols = []
    for j in range(8):
        col = jnp.zeros(shape, jnp.float32)
        for k in range(nodes):
            piece = gram_now[8 * k : 8 * k + 8, 8 * k + j : 8 * k + j + 1]
            col = jnp.where(lane == k, piece, col)
        cols.append(col)
    for _ in range(SUBITERS):
        image = []
        for c in range(STEPS):
            total = cols[0] * basis[c][0:1, :]
            for j in range(1, 8):
                total = total + cols[j] * basis[c][j : j + 1, :]
            image.append(total * live[c])
        inner = {}
        for a in range(STEPS):
            for b in range(a + 1):
                inner[a, b] = sublane_sum(image[a] * image[b])
            inner[a, a] = inner[a, a] + (1.0 - live[a])
        low = {}
        inv = []
        for b in range(STEPS):
            pivot = inner[b, b]
            for k in range(b):
                pivot = pivot - low[b, k] * low[b, k]
            root = lax.rsqrt(pivot)
            root = root * (1.5 - 0.5 * pivot * root * root)
            inv.append(root)
            for a in range(b + 1, STEPS):
                entry = inner[a, b]
                for k in range(b):
                    entry = entry - low[a, k] * low[b, k]
                low[a, b] = entry * root
        fresh = []
        for a in range(STEPS):
            value = image[a]
            for k in range(a):
                value = value - low[a, k] * fresh[k]
            fresh.append(value * inv[a])
        basis = fresh
    return basis


def weights(basis, nodes):
    lane = lane_iota((8, 128))
    rows = []
    for k in range(nodes):
        block = jnp.zeros((8, 128), jnp.float32)
        for c in range(STEPS):
            block = jnp.where(lane == STEPS * k + c, basis[c][:, k : k + 1], block)
        rows.append(block)
    return jnp.concatenate(rows, axis=0) if nodes > 1 else rows[0]


def finish_kernel(start_ref, part_ref, *refs):
    out_ref, w_ref = refs[-2:]
    cores = refs[:STEPS]
    packed = part_ref[0]
    for i in range(1, part_ref.shape[0]):
        packed = packed + part_ref[i]
    size = RUNS * STEPS
    raw = jnp.concatenate(
        [packed if j == 0 else pltpu.roll(packed, 128 - size * j, 1) for j in range(STEPS)], axis=0
    )
    sub = sub_iota((size, 128))
    lane = lane_iota((size, 128))
    raw = jnp.where(lane < size, raw, 0.0)
    perm = jnp.where(lane == 8 * (sub & 3) + (sub >> 2), 1.0, 0.0)
    full = dot(perm[:, :size], raw)
    square = jnp.concatenate([full, jnp.zeros((128 - size, 128), jnp.float32)], axis=0)
    mirror = square.T[:size, :]
    same = ((sub & 3) == (lane & 3)) & (((lane & 16) == 0) | ((sub & 16) != 0))
    full = jnp.where(((sub & 3) < (lane & 3)) | same, full, mirror)
    diag = jnp.where(sub == lane, full, 0.0)
    mu_col = jnp.sum(diag, axis=1, keepdims=True) / CELLS
    mu_row = jnp.sum(diag, axis=0, keepdims=True) / CELLS
    scale_col = 1.0 / jnp.sqrt(mu_col + EPS)
    scale_row = 1.0 / jnp.sqrt(mu_row + EPS)
    gram_now = full * scale_col * scale_row / CELLS
    nodes = RUNS // 2
    level = 0
    total = None
    while nodes:
        basis = level_basis(gram_now, nodes, level, start_ref)
        w = weights(basis, nodes)
        rows_now = 8 * nodes
        total = w if total is None else dot(total[:, :rows_now], w)
        if nodes > 1:
            half = dot(gram_now[:, :rows_now], w)
            w_t = jnp.concatenate([w, jnp.zeros((128 - rows_now, 128), jnp.float32)], axis=0).T
            gram_now = dot(w_t[: STEPS * nodes, :rows_now], half)
        level += 1
        nodes //= 2
    total = total * scale_col
    for c in range(STEPS):
        w_ref[c] = jnp.broadcast_to(total[:, c : c + 1], (size, 128))
    tiles = [slice(8 * i, 8 * i + 8) for i in range(BLOCK // 8)]
    for l in range(NZ // 128):
        cols = slice(128 * l, 128 * l + 128)
        accs = [[None] * len(tiles) for _ in range(STEPS)]
        for q in range(RUNS):
            for t in range(STEPS):
                k = STEPS * q + t
                xs = [cores[t][q, rows, cols] for rows in tiles]
                for c in range(STEPS):
                    weight = jnp.broadcast_to(w_ref[c, k : k + 1, :], (8, 128))
                    for i, x in enumerate(xs):
                        term = weight * x
                        accs[c][i] = term if accs[c][i] is None else accs[c][i] + term
        for c in range(STEPS):
            for i, rows in enumerate(tiles):
                out_ref[c, 0, rows, cols] = accs[c][i]


def finish(start, parts, cores):
    return pl.pallas_call(
        finish_kernel,
        out_shape=jax.ShapeDtypeStruct((STEPS, 1, BLOCK, NZ), jnp.float32),
        in_specs=[VMEM] * (2 + STEPS),
        out_specs=VMEM,
        scratch_shapes=[pltpu.VMEM((STEPS, RUNS * STEPS, 128), jnp.float32)],
        compiler_params=params(),
        cost_estimate=pl.CostEstimate(flops=5000000, bytes_accessed=2400000, transcendentals=0),
        name="finish",
    )(start, parts, *cores)


def local(start_field, viscosity, diffusivity, velocity, assignment, child_order, keep_ranks):
    sibling = [(i, i ^ 1) for i in range(NX)]
    crossing = [(i, i + 1) for i in range(1, NX - 1, 2)] + [(i + 1, i) for i in range(1, NX - 1, 2)]
    blocks = lax.all_to_all(row_blocks(start_field), "run", 0, 0)
    own = assemble(blocks, viscosity)
    table = run_rates(diffusivity, velocity, assignment)
    start = starts(child_order, keep_ranks)
    planes = None
    cores = []
    packed = None

    def swap_cross(a):
        return lax.ppermute(a, SPACE, crossing)

    def swap_sib(a):
        return lax.ppermute(a, SPACE, sibling)

    for turn in range(STEPS // 2):
        sib1 = swap_sib(own)
        cross1 = swap_cross(own)
        if planes is None:
            v, vs1, vc1 = own, sib1, cross1
        acc_own = interior(own, v, table)
        acc_sib = interior(sib1, vs1, table)
        last = turn == STEPS // 2 - 1
        cross2 = swap_cross(trim(sib1) if last else sib1)
        if cores:
            early = (cross1, packed, acc_own)
            cross1, packed, acc_own = lax.optimization_barrier(early)
        else:
            early = (cross1, acc_own, start)
            cross1, acc_own, start = lax.optimization_barrier(early)
        sib2 = swap_sib(trim(cross1) if last else cross1)
        if planes is None:
            planes = vs2, vc2 = sib2, cross2
        acc_cross = interior(cross1, vc1, table)
        fresh, core = close(("full", "core"), acc_own, own, sib1, cross1, v, vs1, vc1, table)
        cores.append(core)
        packed = gram(cores, packed, False)
        (near_sib,) = close(("full",), acc_sib, sib1, sib2, own, vs1, vs2, v, table)
        acc_own = interior(fresh, v, table)
        (near_cross,) = close(("full",), acc_cross, cross1, own, cross2, vc1, v, vc2, table, edge=True)
        want = ("core",) if last else ("full", "core")
        result = close(want, acc_own, fresh, near_sib, near_cross, v, vs1, vc1, table)
        cores.append(result[-1])
        own = result[0]
        if not last:
            packed = gram(cores, packed, False)
    parts = gram(cores, packed, True)
    parts = spread(lax.all_to_all(parts, ("y", "core"), 0, 0))
    parts = lax.all_to_all(parts, ("run", "x"), 0, 0)
    return finish(start, parts, cores)


def solution(mesh):
    fine = Mesh(mesh.devices.reshape(8, 4, 8, 2), ("run", "x", "y", "core"))
    in_specs = (P("run", SPACE, None, None), P(SPACE, None, None), P(), P(), P(), P(), P())
    out_specs = P(None, SPACE, "run", None)
    return jax.shard_map(local, mesh=fine, in_specs=in_specs, out_specs=out_specs, check_vma=False)
```

```python
import math

import jax
import jax.numpy as jnp
from jax import lax
from jax.experimental import pallas as pl
from jax.experimental.pallas import tpu as pltpu
from jax.sharding import Mesh, PartitionSpec as P

STEPS = 4
SUBITERS = 3
EPS = 1e-06
RUNS = 8
NY = 256
NZ = 512
NX = 64
BLOCK = NY // RUNS
HALO = STEPS
EXT = BLOCK + 2 * HALO
CELLS = NX * NY * NZ
EXACT = lax.Precision.HIGHEST
SPACE = ("x", "y", "core")
FIRST = 16
SECOND = 32
VMEM = pl.BlockSpec(memory_space=pltpu.VMEM)
SMEM = pl.BlockSpec(memory_space=pltpu.SMEM)


def sub_iota(shape):
    return lax.broadcasted_iota(jnp.int32, shape, 0)


def lane_iota(shape):
    return lax.broadcasted_iota(jnp.int32, shape, 1)


def params(limit=40 << 20):
    return pltpu.CompilerParams(vmem_limit_bytes=limit)


ROWS = 8
TILES = NY // 8


def shifted(before, after):
    low = sub_iota((8, NZ)) < 4
    return pltpu.roll(jnp.where(low, after, before), 4, 0)


def blocks_kernel(field_ref, out_ref):
    zero = jnp.zeros((8, NZ), jnp.float32)
    before = zero
    for m in range(TILES + 1):
        after = field_ref[0, 0, 8 * m : 8 * m + 8, :] if m < TILES else zero
        tile = shifted(before, after)
        before = after
        for q in range(RUNS):
            j = m - 4 * q
            if 0 <= j <= 4:
                out_ref[q, 8 * j : 8 * j + 8, :] = tile


def row_blocks(field):
    return pl.pallas_call(
        blocks_kernel,
        out_shape=jax.ShapeDtypeStruct((RUNS, EXT, NZ), jnp.float32),
        in_specs=[VMEM],
        out_specs=VMEM,
        compiler_params=params(),
        cost_estimate=pl.CostEstimate(flops=200000, bytes_accessed=1200000, transcendentals=0),
        name="row_blocks",
    )(field)


def rates_kernel(diff_ref, vel_ref, assign_ref, table_ref):
    even = lax.axis_index("core") == 0
    for q in range(RUNS):
        s = assign_ref[q]
        ups = [-jnp.minimum(vel_ref[d, s], 0.0) for d in range(3)]
        downs = [jnp.maximum(vel_ref[d, s], 0.0) for d in range(3)]
        w_sib = jnp.where(even, ups[0], downs[0])
        w_cross = jnp.where(even, downs[0], ups[0])
        values = (0.5 * diff_ref[s], w_sib, w_cross, ups[1], downs[1], ups[2], downs[2])
        for k, value in enumerate(values):
            table_ref[ROWS * q + k : ROWS * q + k + 1, :] = jnp.full((1, NZ), value, jnp.float32)


def run_rates(diffusivity, velocity, assignment):
    return pl.pallas_call(
        rates_kernel,
        out_shape=jax.ShapeDtypeStruct((ROWS * RUNS, NZ), jnp.float32),
        in_specs=[SMEM, SMEM, SMEM],
        out_specs=VMEM,
        compiler_params=params(),
        cost_estimate=pl.CostEstimate(flops=0, bytes_accessed=140000, transcendentals=0),
        name="rates",
    )(diffusivity, velocity.T, assignment)


def assemble_kernel(state_ref, visc_ref, out_ref):
    run = lax.axis_index("run")
    for q in range(RUNS):
        out_ref[q] = state_ref[q]
    for j in range(5):
        m = 4 * run + j
        prev_at = pl.multiple_of(8 * jnp.maximum(m - 1, 0), 8)
        next_at = pl.multiple_of(8 * jnp.minimum(m, TILES - 1), 8)
        prev = jnp.where(m > 0, visc_ref[0, pl.ds(prev_at, 8), :], 0.0)
        nxt = jnp.where(m < TILES, visc_ref[0, pl.ds(next_at, 8), :], 0.0)
        out_ref[RUNS, 8 * j : 8 * j + 8, :] = shifted(prev, nxt)


def assemble(state, visc):
    return pl.pallas_call(
        assemble_kernel,
        out_shape=jax.ShapeDtypeStruct((RUNS + 1, EXT, NZ), jnp.float32),
        in_specs=[VMEM, VMEM],
        out_specs=VMEM,
        compiler_params=params(),
        cost_estimate=pl.CostEstimate(flops=0, bytes_accessed=1400000, transcendentals=0),
        name="assemble",
    )(state, visc)


def trim_kernel(in_ref, out_ref):
    for q in range(RUNS):
        out_ref[q] = pltpu.roll(in_ref[q], EXT - HALO, 0)[:BLOCK]


def trim(plane):
    return pl.pallas_call(
        trim_kernel,
        out_shape=jax.ShapeDtypeStruct((RUNS, BLOCK, NZ), jnp.float32),
        in_specs=[VMEM],
        out_specs=VMEM,
        compiler_params=params(),
        cost_estimate=pl.CostEstimate(flops=0, bytes_accessed=1200000, transcendentals=0),
        name="trim",
    )(plane)


def interior_kernel(u_ref, v_ref, table_ref, out_ref):
    col = lane_iota((EXT, NZ))
    first_col = col == 0
    last_col = col == NZ - 1
    v = v_ref[RUNS]

    def ahead_row(a):
        return pltpu.roll(a, EXT - 1, 0)

    def behind_row(a):
        return pltpu.roll(a, 1, 0)

    def ahead_col(a):
        return jnp.where(last_col, 0.0, pltpu.roll(a, NZ - 1, 1))

    def behind_col(a):
        return jnp.where(first_col, 0.0, pltpu.roll(a, 1, 1))

    moves = (ahead_row, behind_row, ahead_col, behind_col)
    coefs = [v + move(v) for move in moves]
    for q in range(RUNS):
        u = u_ref[q]
        rates = [table_ref[ROWS * q + k : ROWS * q + k + 1, :] for k in range(7)]
        new = u
        for k, move in enumerate(moves):
            new = new + (rates[0] * coefs[k] + rates[3 + k]) * (move(u) - u)
        out_ref[q] = new


def interior(state, visc, table):
    return pl.pallas_call(
        interior_kernel,
        out_shape=jax.ShapeDtypeStruct((RUNS, EXT, NZ), jnp.float32),
        in_specs=[VMEM] * 3,
        out_specs=VMEM,
        compiler_params=params(),
        cost_estimate=pl.CostEstimate(flops=4000000, bytes_accessed=1400000, transcendentals=0),
        name="interior",
    )(state, visc, table)


def padded(rows):
    if rows.shape[0] == EXT:
        return rows
    return pltpu.roll(jnp.concatenate([rows, jnp.zeros((2 * HALO, NZ), jnp.float32)], axis=0), HALO, 0)


def close_kernel(edge, want, acc_ref, u_ref, sib_ref, cross_ref, v_ref, vs_ref, vc_ref, table_ref, *outs):
    run = lax.axis_index("run")
    row = sub_iota((EXT, NZ)) + (BLOCK * run - HALO)
    inside = (row >= 0) & (row < NY)
    if edge:
        place = (lax.axis_index("x") * 8 + lax.axis_index("y")) * 2 + lax.axis_index("core")
        inside = inside & (place > 0) & (place < NX - 1)
    v = v_ref[RUNS]
    c_sib = v + vs_ref[RUNS]
    c_cross = v + vc_ref[RUNS]
    for q in range(RUNS):
        rates = [table_ref[ROWS * q + k : ROWS * q + k + 1, :] for k in range(3)]
        u = u_ref[q]
        new = acc_ref[q] + (rates[0] * c_sib + rates[1]) * (padded(sib_ref[q]) - u)
        across = padded(cross_ref[q])
        new = new + (rates[0] * c_cross + rates[2]) * (across - u)
        new = jnp.where(inside, new, 0.0)
        if "full" in want:
            outs[0][q] = new
        if "core" in want:
            outs[-1][q] = pltpu.roll(new, EXT - HALO, 0)[:BLOCK]


def close(want, acc, u, sib, cross, v, v_sib, v_cross, table, edge=False):
    sizes = [EXT] * ("full" in want) + [BLOCK] * ("core" in want)
    args = [acc, u, sib, cross, v, v_sib, v_cross, table]

    def body(*refs):
        close_kernel(edge, want, *refs)

    return pl.pallas_call(
        body,
        out_shape=tuple(jax.ShapeDtypeStruct((RUNS, rows, NZ), jnp.float32) for rows in sizes),
        in_specs=[VMEM] * len(args),
        out_specs=tuple(VMEM for _ in sizes),
        compiler_params=params(),
        cost_estimate=pl.CostEstimate(flops=1200000, bytes_accessed=1600000, transcendentals=0),
        name="close_" + "_".join(want),
    )(*args)


def merge(x, y, width):
    sub = sub_iota((8, 128))
    pick = (sub & width) == 0
    keep = jnp.where(pick, x, y)
    give = jnp.where(pick, y, x)
    if width == 4:
        moved = pltpu.roll(give, 4, 0)
    else:
        moved = jnp.where(pick, pltpu.roll(give, 8 - width, 0), pltpu.roll(give, width, 0))
    return keep + moved


def gram_kernel(group, last, *refs):
    cores = refs[: group + 1]
    prev_ref = refs[group + 1] if group else None
    out_ref = refs[-1]
    mine = cores[group]
    lane = lane_iota((8, 128))
    packed = prev_ref[...] if group else jnp.zeros((8, 128), jnp.float32)
    for other in range(group + 1):
        theirs = cores[other]
        for half in range(2):
            first = 4 if other == group and half else 0
            wide = 8 - first
            accs = tuple(jnp.zeros((8, 128), jnp.float32) for _ in range(4 * wide))

            def body(i, accs, theirs=theirs, half=half, first=first, wide=wide):
                rows = slice(8 * i, 8 * i + 8)
                accs = list(accs)
                for l in range(NZ // 128):
                    cols = slice(128 * l, 128 * l + 128)
                    a = [mine[4 * half + k, rows, cols] for k in range(4)]
                    for b in range(wide):
                        t = theirs[first + b, rows, cols]
                        for k in range(4):
                            accs[wide * k + b] = accs[wide * k + b] + a[k] * t
                return tuple(accs)

            for i in range(BLOCK // 8):
                accs = body(i, accs)
            for k in range(4):
                level = [jnp.zeros((8, 128), jnp.float32)] * first + list(accs[wide * k : wide * k + wide])
                for width in (4, 2, 1):
                    count = len(level) // 2
                    level = [merge(level[i], level[i + count], width) for i in range(count)]
                total = jnp.sum(level[0], axis=1, keepdims=True)
                at = 32 * other + STEPS * (4 * half + k) + group
                packed = jnp.where(lane == at, total, packed)
    if last:
        for i in range(FIRST):
            out_ref[i] = packed
    else:
        out_ref[...] = packed


def gram(cores, prev, last):
    group = len(cores) - 1
    shape = (FIRST, 8, 128) if last else (8, 128)
    args = list(cores) + ([prev] if group else [])

    def body(*refs):
        gram_kernel(group, last, *refs)

    return pl.pallas_call(
        body,
        out_shape=jax.ShapeDtypeStruct(shape, jnp.float32),
        in_specs=[VMEM] * len(args),
        out_specs=VMEM,
        compiler_params=params(),
        cost_estimate=pl.CostEstimate(flops=2200000 * (group + 1), bytes_accessed=600000 * (group + 1), transcendentals=0),
        name=f"gram{group}",
    )(*args)


def spread_kernel(in_ref, out_ref):
    total = in_ref[0]
    for i in range(1, FIRST):
        total = total + in_ref[i]
    for i in range(SECOND):
        out_ref[i] = total


def spread(parts):
    return pl.pallas_call(
        spread_kernel,
        out_shape=jax.ShapeDtypeStruct((SECOND, 8, 128), jnp.float32),
        in_specs=[VMEM],
        out_specs=VMEM,
        compiler_params=params(),
        name="spread",
    )(parts)


def dot(a, b):
    return jnp.dot(a, b, precision=EXACT, preferred_element_type=jnp.float32)


def dct():
    size = 2 * STEPS
    return [
        [math.sqrt(1.0 / STEPS) * math.cos(math.pi * (i + 0.5) * (j + 0.5) / size) for j in range(STEPS)]
        for i in range(size)
    ]


def sublane_sum(a):
    for width in (4, 2, 1):
        a = a + pltpu.roll(a, width, 0)
    return a


def starts_kernel(order_ref, keep_ref, out_ref):
    shape = (8, 128)
    sub = sub_iota(shape)
    table = dct()
    nodes = RUNS // 2
    first_node = 0
    level = 0
    while nodes:
        lane = lane_iota(shape) & (nodes - 1)
        basis = [jnp.zeros(shape, jnp.float32) for _ in range(STEPS)]
        live = [jnp.zeros(shape, jnp.float32) for _ in range(STEPS)]
        for k in range(nodes):
            node = first_node + k
            here = lane == k
            for c in range(STEPS):
                flag = jnp.where(keep_ref[node] > c, 1.0, 0.0)
                live[c] = jnp.where(here, flag, live[c])
            for i in range(2 * STEPS):
                spot = here & (sub == order_ref[node, i])
                for c in range(STEPS):
                    basis[c] = jnp.where(spot, table[i][c], basis[c])
        for c in range(STEPS):
            out_ref[2 * STEPS * level + c] = basis[c] * live[c]
            out_ref[2 * STEPS * level + STEPS + c] = live[c]
        first_node += nodes
        nodes //= 2
        level += 1


def starts(order, keep):
    return pl.pallas_call(
        starts_kernel,
        out_shape=jax.ShapeDtypeStruct((3 * 2 * STEPS, 8, 128), jnp.float32),
        in_specs=[SMEM, SMEM],
        out_specs=VMEM,
        compiler_params=params(),
        cost_estimate=pl.CostEstimate(flops=0, bytes_accessed=100000, transcendentals=0),
        name="starts",
    )(order, keep)


def level_basis(gram_now, nodes, level, start_ref):
    shape = (8, 128)
    lane = lane_iota(shape) & (nodes - 1)
    basis = [start_ref[2 * STEPS * level + c] for c in range(STEPS)]
    live = [start_ref[2 * STEPS * level + STEPS + c] for c in range(STEPS)]
    cols = []
    for j in range(8):
        col = jnp.zeros(shape, jnp.float32)
        for k in range(nodes):
            piece = gram_now[8 * k : 8 * k + 8, 8 * k + j : 8 * k + j + 1]
            col = jnp.where(lane == k, piece, col)
        cols.append(col)
    for _ in range(SUBITERS):
        image = []
        for c in range(STEPS):
            total = cols[0] * basis[c][0:1, :]
            for j in range(1, 8):
                total = total + cols[j] * basis[c][j : j + 1, :]
            image.append(total * live[c])
        inner = {}
        for a in range(STEPS):
            for b in range(a + 1):
                inner[a, b] = sublane_sum(image[a] * image[b])
            inner[a, a] = inner[a, a] + (1.0 - live[a])
        low = {}
        inv = []
        for b in range(STEPS):
            pivot = inner[b, b]
            for k in range(b):
                pivot = pivot - low[b, k] * low[b, k]
            root = lax.rsqrt(pivot)
            root = root * (1.5 - 0.5 * pivot * root * root)
            inv.append(root)
            for a in range(b + 1, STEPS):
                entry = inner[a, b]
                for k in range(b):
                    entry = entry - low[a, k] * low[b, k]
                low[a, b] = entry * root
        fresh = []
        for a in range(STEPS):
            value = image[a]
            for k in range(a):
                value = value - low[a, k] * fresh[k]
            fresh.append(value * inv[a])
        basis = fresh
    return basis


def weights(basis, nodes):
    lane = lane_iota((8, 128))
    rows = []
    for k in range(nodes):
        block = jnp.zeros((8, 128), jnp.float32)
        for c in range(STEPS):
            block = jnp.where(lane == STEPS * k + c, basis[c][:, k : k + 1], block)
        rows.append(block)
    return jnp.concatenate(rows, axis=0) if nodes > 1 else rows[0]


def finish_kernel(start_ref, part_ref, *refs):
    out_ref, w_ref = refs[-2:]
    cores = refs[:STEPS]
    packed = part_ref[0]
    for i in range(1, part_ref.shape[0]):
        packed = packed + part_ref[i]
    size = RUNS * STEPS
    raw = jnp.concatenate(
        [packed if j == 0 else pltpu.roll(packed, 128 - size * j, 1) for j in range(STEPS)], axis=0
    )
    sub = sub_iota((size, 128))
    lane = lane_iota((size, 128))
    raw = jnp.where(lane < size, raw, 0.0)
    eight = sub_iota((8, 128))
    blocks = []
    for m in range(STEPS):
        block = jnp.zeros((8, 128), jnp.float32)
        for r in range(8):
            at = 8 * (r & 3) + 2 * m + (r >> 2)
            block = jnp.where(eight == r, raw[at : at + 1, :], block)
        blocks.append(block)
    full = jnp.concatenate(blocks, axis=0)
    square = jnp.concatenate([full, jnp.zeros((128 - size, 128), jnp.float32)], axis=0)
    mirror = square.T[:size, :]
    same = ((sub & 3) == (lane & 3)) & (((lane & 16) == 0) | ((sub & 16) != 0))
    full = jnp.where(((sub & 3) < (lane & 3)) | same, full, mirror)
    diag = jnp.where(sub == lane, full, 0.0)
    mu_col = jnp.sum(diag, axis=1, keepdims=True) / CELLS
    mu_row = jnp.sum(diag, axis=0, keepdims=True) / CELLS
    scale_col = 1.0 / jnp.sqrt(mu_col + EPS)
    scale_row = 1.0 / jnp.sqrt(mu_row + EPS)
    gram_now = full * scale_col * scale_row / CELLS
    nodes = RUNS // 2
    level = 0
    total = None
    while nodes:
        basis = level_basis(gram_now, nodes, level, start_ref)
        w = weights(basis, nodes)
        rows_now = 8 * nodes
        total = w if total is None else dot(total[:, :rows_now], w)
        if nodes > 1:
            half = dot(gram_now[:, :rows_now], w)
            rows = []
            for b in range(nodes // 2):
                block = jnp.zeros((8, 128), jnp.float32)
                for r in range(8):
                    k = 2 * b + (r >> 2)
                    column = basis[r & 3][:, k : k + 1]
                    row = sublane_sum(column * half[8 * k : 8 * k + 8, :])
                    block = jnp.where(eight == r, row, block)
                rows.append(block)
            gram_now = jnp.concatenate(rows, axis=0) if len(rows) > 1 else rows[0]
        level += 1
        nodes //= 2
    total = total * scale_col
    for c in range(STEPS):
        w_ref[c] = jnp.broadcast_to(total[:, c : c + 1], (size, 128))
    tiles = [slice(8 * i, 8 * i + 8) for i in range(BLOCK // 8)]
    for l in range(NZ // 128):
        cols = slice(128 * l, 128 * l + 128)
        accs = [[None] * len(tiles) for _ in range(STEPS)]
        for q in range(RUNS):
            for t in range(STEPS):
                k = STEPS * q + t
                xs = [cores[t][q, rows, cols] for rows in tiles]
                for c in range(STEPS):
                    weight = jnp.broadcast_to(w_ref[c, k : k + 1, :], (8, 128))
                    for i, x in enumerate(xs):
                        term = weight * x
                        accs[c][i] = term if accs[c][i] is None else accs[c][i] + term
        for c in range(STEPS):
            for i, rows in enumerate(tiles):
                out_ref[c, 0, rows, cols] = accs[c][i]


def finish(start, parts, cores):
    return pl.pallas_call(
        finish_kernel,
        out_shape=jax.ShapeDtypeStruct((STEPS, 1, BLOCK, NZ), jnp.float32),
        in_specs=[VMEM] * (2 + STEPS),
        out_specs=VMEM,
        scratch_shapes=[pltpu.VMEM((STEPS, RUNS * STEPS, 128), jnp.float32)],
        compiler_params=params(),
        cost_estimate=pl.CostEstimate(flops=5000000, bytes_accessed=2400000, transcendentals=0),
        name="finish",
    )(start, parts, *cores)


def local(start_field, viscosity, diffusivity, velocity, assignment, child_order, keep_ranks):
    sibling = [(i, i ^ 1) for i in range(NX)]
    crossing = [(i, i + 1) for i in range(1, NX - 1, 2)] + [(i + 1, i) for i in range(1, NX - 1, 2)]
    blocks = lax.all_to_all(row_blocks(start_field), "run", 0, 0)
    own = assemble(blocks, viscosity)
    table = run_rates(diffusivity, velocity, assignment)
    start = starts(child_order, keep_ranks)
    planes = None
    cores = []
    packed = None

    def swap_cross(a):
        return lax.ppermute(a, SPACE, crossing)

    def swap_sib(a):
        return lax.ppermute(a, SPACE, sibling)

    for turn in range(STEPS // 2):
        sib1 = swap_sib(own)
        cross1 = swap_cross(own)
        if planes is None:
            v, vs1, vc1 = own, sib1, cross1
        acc_own = interior(own, v, table)
        acc_sib = interior(sib1, vs1, table)
        last = turn == STEPS // 2 - 1
        cross2 = swap_cross(trim(sib1) if last else sib1)
        if cores:
            early = (cross1, packed, acc_own)
            cross1, packed, acc_own = lax.optimization_barrier(early)
        else:
            early = (cross1, acc_own, acc_sib, start)
            cross1, acc_own, acc_sib, start = lax.optimization_barrier(early)
        sib2 = swap_sib(trim(cross1) if last else cross1)
        if planes is None:
            planes = vs2, vc2 = sib2, cross2
        acc_cross = interior(cross1, vc1, table)
        fresh, core = close(("full", "core"), acc_own, own, sib1, cross1, v, vs1, vc1, table)
        cores.append(core)
        packed = gram(cores, packed, False)
        (near_sib,) = close(("full",), acc_sib, sib1, sib2, own, vs1, vs2, v, table)
        acc_own = interior(fresh, v, table)
        (near_cross,) = close(("full",), acc_cross, cross1, own, cross2, vc1, v, vc2, table, edge=True)
        want = ("core",) if last else ("full", "core")
        result = close(want, acc_own, fresh, near_sib, near_cross, v, vs1, vc1, table)
        cores.append(result[-1])
        own = result[0]
        if not last:
            packed = gram(cores, packed, False)
    parts = gram(cores, packed, True)
    parts = spread(lax.all_to_all(parts, ("y", "core"), 0, 0))
    parts = lax.all_to_all(parts, ("run", "x"), 0, 0)
    return finish(start, parts, cores)


def solution(mesh):
    fine = Mesh(mesh.devices.reshape(8, 4, 8, 2), ("run", "x", "y", "core"))
    in_specs = (P("run", SPACE, None, None), P(SPACE, None, None), P(), P(), P(), P(), P())
    out_specs = P(None, SPACE, "run", None)
    return jax.shard_map(local, mesh=fine, in_specs=in_specs, out_specs=out_specs, check_vma=False)
```

```python
import math

import jax
import jax.numpy as jnp
from jax import lax
from jax.experimental import pallas as pl
from jax.experimental.pallas import tpu as pltpu
from jax.sharding import Mesh, PartitionSpec as P

STEPS = 4
SUBITERS = 3
EPS = 1e-06
RUNS = 8
NY = 256
NZ = 512
NX = 64
BLOCK = NY // RUNS
HALO = STEPS
EXT = BLOCK + 2 * HALO
CELLS = NX * NY * NZ
EXACT = lax.Precision.HIGHEST
SPACE = ("x", "y", "core")
FIRST = 16
SECOND = 32
VMEM = pl.BlockSpec(memory_space=pltpu.VMEM)
SMEM = pl.BlockSpec(memory_space=pltpu.SMEM)


def sub_iota(shape):
    return lax.broadcasted_iota(jnp.int32, shape, 0)


def lane_iota(shape):
    return lax.broadcasted_iota(jnp.int32, shape, 1)


def params(limit=40 << 20):
    return pltpu.CompilerParams(vmem_limit_bytes=limit)


ROWS = 8
TILES = NY // 8


def shifted(before, after):
    low = sub_iota((8, NZ)) < 4
    return pltpu.roll(jnp.where(low, after, before), 4, 0)


def blocks_kernel(field_ref, out_ref):
    zero = jnp.zeros((8, NZ), jnp.float32)
    before = zero
    for m in range(TILES + 1):
        after = field_ref[0, 0, 8 * m : 8 * m + 8, :] if m < TILES else zero
        tile = shifted(before, after)
        before = after
        for q in range(RUNS):
            j = m - 4 * q
            if 0 <= j <= 4:
                out_ref[q, 8 * j : 8 * j + 8, :] = tile


def row_blocks(field):
    return pl.pallas_call(
        blocks_kernel,
        out_shape=jax.ShapeDtypeStruct((RUNS, EXT, NZ), jnp.float32),
        in_specs=[VMEM],
        out_specs=VMEM,
        compiler_params=params(),
        cost_estimate=pl.CostEstimate(flops=200000, bytes_accessed=1200000, transcendentals=0),
        name="row_blocks",
    )(field)


def rates_kernel(diff_ref, vel_ref, assign_ref, table_ref):
    even = lax.axis_index("core") == 0
    for q in range(RUNS):
        s = assign_ref[q]
        ups = [-jnp.minimum(vel_ref[d, s], 0.0) for d in range(3)]
        downs = [jnp.maximum(vel_ref[d, s], 0.0) for d in range(3)]
        w_sib = jnp.where(even, ups[0], downs[0])
        w_cross = jnp.where(even, downs[0], ups[0])
        values = (0.5 * diff_ref[s], w_sib, w_cross, ups[1], downs[1], ups[2], downs[2])
        for k, value in enumerate(values):
            table_ref[ROWS * q + k : ROWS * q + k + 1, :] = jnp.full((1, NZ), value, jnp.float32)


def run_rates(diffusivity, velocity, assignment):
    return pl.pallas_call(
        rates_kernel,
        out_shape=jax.ShapeDtypeStruct((ROWS * RUNS, NZ), jnp.float32),
        in_specs=[SMEM, SMEM, SMEM],
        out_specs=VMEM,
        compiler_params=params(),
        cost_estimate=pl.CostEstimate(flops=0, bytes_accessed=140000, transcendentals=0),
        name="rates",
    )(diffusivity, velocity.T, assignment)


def assemble_kernel(state_ref, visc_ref, out_ref):
    run = lax.axis_index("run")
    for q in range(RUNS):
        out_ref[q] = state_ref[q]
    for j in range(5):
        m = 4 * run + j
        prev_at = pl.multiple_of(8 * jnp.maximum(m - 1, 0), 8)
        next_at = pl.multiple_of(8 * jnp.minimum(m, TILES - 1), 8)
        prev = jnp.where(m > 0, visc_ref[0, pl.ds(prev_at, 8), :], 0.0)
        nxt = jnp.where(m < TILES, visc_ref[0, pl.ds(next_at, 8), :], 0.0)
        out_ref[RUNS, 8 * j : 8 * j + 8, :] = shifted(prev, nxt)


def assemble(state, visc):
    return pl.pallas_call(
        assemble_kernel,
        out_shape=jax.ShapeDtypeStruct((RUNS + 1, EXT, NZ), jnp.float32),
        in_specs=[VMEM, VMEM],
        out_specs=VMEM,
        compiler_params=params(),
        cost_estimate=pl.CostEstimate(flops=0, bytes_accessed=1400000, transcendentals=0),
        name="assemble",
    )(state, visc)


def trim_kernel(in_ref, out_ref):
    for q in range(RUNS):
        out_ref[q] = pltpu.roll(in_ref[q], EXT - HALO, 0)[:BLOCK]


def trim(plane):
    return pl.pallas_call(
        trim_kernel,
        out_shape=jax.ShapeDtypeStruct((RUNS, BLOCK, NZ), jnp.float32),
        in_specs=[VMEM],
        out_specs=VMEM,
        compiler_params=params(),
        cost_estimate=pl.CostEstimate(flops=0, bytes_accessed=1200000, transcendentals=0),
        name="trim",
    )(plane)


def interior_kernel(u_ref, v_ref, table_ref, out_ref):
    col = lane_iota((EXT, NZ))
    first_col = col == 0
    last_col = col == NZ - 1
    v = v_ref[RUNS]

    def ahead_row(a):
        return pltpu.roll(a, EXT - 1, 0)

    def behind_row(a):
        return pltpu.roll(a, 1, 0)

    def ahead_col(a):
        return jnp.where(last_col, 0.0, pltpu.roll(a, NZ - 1, 1))

    def behind_col(a):
        return jnp.where(first_col, 0.0, pltpu.roll(a, 1, 1))

    moves = (ahead_row, behind_row, ahead_col, behind_col)
    coefs = [v + move(v) for move in moves]
    for q in range(RUNS):
        u = u_ref[q]
        rates = [table_ref[ROWS * q + k : ROWS * q + k + 1, :] for k in range(7)]
        new = u
        for k, move in enumerate(moves):
            new = new + (rates[0] * coefs[k] + rates[3 + k]) * (move(u) - u)
        out_ref[q] = new


def interior(state, visc, table):
    return pl.pallas_call(
        interior_kernel,
        out_shape=jax.ShapeDtypeStruct((RUNS, EXT, NZ), jnp.float32),
        in_specs=[VMEM] * 3,
        out_specs=VMEM,
        compiler_params=params(),
        cost_estimate=pl.CostEstimate(flops=4000000, bytes_accessed=1400000, transcendentals=0),
        name="interior",
    )(state, visc, table)


def padded(rows):
    if rows.shape[0] == EXT:
        return rows
    return pltpu.roll(jnp.concatenate([rows, jnp.zeros((2 * HALO, NZ), jnp.float32)], axis=0), HALO, 0)


def close_kernel(edge, want, acc_ref, u_ref, sib_ref, cross_ref, v_ref, vs_ref, vc_ref, table_ref, *outs):
    run = lax.axis_index("run")
    row = sub_iota((EXT, NZ)) + (BLOCK * run - HALO)
    inside = (row >= 0) & (row < NY)
    if edge:
        place = (lax.axis_index("x") * 8 + lax.axis_index("y")) * 2 + lax.axis_index("core")
        inside = inside & (place > 0) & (place < NX - 1)
    v = v_ref[RUNS]
    c_sib = v + vs_ref[RUNS]
    c_cross = v + vc_ref[RUNS]
    for q in range(RUNS):
        rates = [table_ref[ROWS * q + k : ROWS * q + k + 1, :] for k in range(3)]
        u = u_ref[q]
        new = acc_ref[q] + (rates[0] * c_sib + rates[1]) * (padded(sib_ref[q]) - u)
        across = padded(cross_ref[q])
        new = new + (rates[0] * c_cross + rates[2]) * (across - u)
        new = jnp.where(inside, new, 0.0)
        if "full" in want:
            outs[0][q] = new
        if "core" in want:
            outs[-1][q] = pltpu.roll(new, EXT - HALO, 0)[:BLOCK]


def close(want, acc, u, sib, cross, v, v_sib, v_cross, table, edge=False):
    sizes = [EXT] * ("full" in want) + [BLOCK] * ("core" in want)
    args = [acc, u, sib, cross, v, v_sib, v_cross, table]

    def body(*refs):
        close_kernel(edge, want, *refs)

    return pl.pallas_call(
        body,
        out_shape=tuple(jax.ShapeDtypeStruct((RUNS, rows, NZ), jnp.float32) for rows in sizes),
        in_specs=[VMEM] * len(args),
        out_specs=tuple(VMEM for _ in sizes),
        compiler_params=params(),
        cost_estimate=pl.CostEstimate(flops=1200000, bytes_accessed=1600000, transcendentals=0),
        name="close_" + "_".join(want),
    )(*args)


def merge(x, y, width):
    sub = sub_iota((8, 128))
    pick = (sub & width) == 0
    keep = jnp.where(pick, x, y)
    give = jnp.where(pick, y, x)
    if width == 4:
        moved = pltpu.roll(give, 4, 0)
    else:
        moved = jnp.where(pick, pltpu.roll(give, 8 - width, 0), pltpu.roll(give, width, 0))
    return keep + moved


def gram_kernel(group, last, *refs):
    cores = refs[: group + 1]
    prev_ref = refs[group + 1] if group else None
    out_ref = refs[-1]
    mine = cores[group]
    lane = lane_iota((8, 128))
    packed = prev_ref[...] if group else jnp.zeros((8, 128), jnp.float32)
    for other in range(group + 1):
        theirs = cores[other]
        for half in range(2):
            first = 4 if other == group and half else 0
            wide = 8 - first
            accs = tuple(jnp.zeros((8, 128), jnp.float32) for _ in range(4 * wide))

            def body(i, accs, theirs=theirs, half=half, first=first, wide=wide):
                rows = slice(8 * i, 8 * i + 8)
                accs = list(accs)
                for l in range(NZ // 128):
                    cols = slice(128 * l, 128 * l + 128)
                    a = [mine[4 * half + k, rows, cols] for k in range(4)]
                    for b in range(wide):
                        t = theirs[first + b, rows, cols]
                        for k in range(4):
                            accs[wide * k + b] = accs[wide * k + b] + a[k] * t
                return tuple(accs)

            for i in range(BLOCK // 8):
                accs = body(i, accs)
            for k in range(4):
                level = [jnp.zeros((8, 128), jnp.float32)] * first + list(accs[wide * k : wide * k + wide])
                for width in (4, 2, 1):
                    count = len(level) // 2
                    level = [merge(level[i], level[i + count], width) for i in range(count)]
                total = jnp.sum(level[0], axis=1, keepdims=True)
                at = 32 * other + STEPS * (4 * half + k) + group
                packed = jnp.where(lane == at, total, packed)
    if last:
        for i in range(FIRST):
            out_ref[i] = packed
    else:
        out_ref[...] = packed


def gram(cores, prev, last):
    group = len(cores) - 1
    shape = (FIRST, 8, 128) if last else (8, 128)
    args = list(cores) + ([prev] if group else [])

    def body(*refs):
        gram_kernel(group, last, *refs)

    return pl.pallas_call(
        body,
        out_shape=jax.ShapeDtypeStruct(shape, jnp.float32),
        in_specs=[VMEM] * len(args),
        out_specs=VMEM,
        compiler_params=params(),
        cost_estimate=pl.CostEstimate(flops=2200000 * (group + 1), bytes_accessed=600000 * (group + 1), transcendentals=0),
        name=f"gram{group}",
    )(*args)


def spread_kernel(in_ref, out_ref):
    total = in_ref[0]
    for i in range(1, FIRST):
        total = total + in_ref[i]
    for i in range(SECOND):
        out_ref[i] = total


def spread(parts):
    return pl.pallas_call(
        spread_kernel,
        out_shape=jax.ShapeDtypeStruct((SECOND, 8, 128), jnp.float32),
        in_specs=[VMEM],
        out_specs=VMEM,
        compiler_params=params(),
        name="spread",
    )(parts)


def dot(a, b):
    return jnp.dot(a, b, precision=EXACT, preferred_element_type=jnp.float32)


def dct():
    size = 2 * STEPS
    return [
        [math.sqrt(1.0 / STEPS) * math.cos(math.pi * (i + 0.5) * (j + 0.5) / size) for j in range(STEPS)]
        for i in range(size)
    ]


def sublane_sum(a):
    for width in (4, 2, 1):
        a = a + pltpu.roll(a, width, 0)
    return a


def starts_kernel(order_ref, keep_ref, out_ref):
    shape = (8, 128)
    sub = sub_iota(shape)
    table = dct()
    nodes = RUNS // 2
    first_node = 0
    level = 0
    while nodes:
        lane = lane_iota(shape) & (nodes - 1)
        basis = [jnp.zeros(shape, jnp.float32) for _ in range(STEPS)]
        live = [jnp.zeros(shape, jnp.float32) for _ in range(STEPS)]
        for k in range(nodes):
            node = first_node + k
            here = lane == k
            for c in range(STEPS):
                flag = jnp.where(keep_ref[node] > c, 1.0, 0.0)
                live[c] = jnp.where(here, flag, live[c])
            for i in range(2 * STEPS):
                spot = here & (sub == order_ref[node, i])
                for c in range(STEPS):
                    basis[c] = jnp.where(spot, table[i][c], basis[c])
        for c in range(STEPS):
            out_ref[2 * STEPS * level + c] = basis[c] * live[c]
            out_ref[2 * STEPS * level + STEPS + c] = live[c]
        first_node += nodes
        nodes //= 2
        level += 1


def starts(order, keep):
    return pl.pallas_call(
        starts_kernel,
        out_shape=jax.ShapeDtypeStruct((3 * 2 * STEPS, 8, 128), jnp.float32),
        in_specs=[SMEM, SMEM],
        out_specs=VMEM,
        compiler_params=params(),
        cost_estimate=pl.CostEstimate(flops=0, bytes_accessed=100000, transcendentals=0),
        name="starts",
    )(order, keep)


def level_basis(gram_now, nodes, level, start_ref):
    shape = (8, 128)
    lane = lane_iota(shape) & (nodes - 1)
    basis = [start_ref[2 * STEPS * level + c] for c in range(STEPS)]
    live = [start_ref[2 * STEPS * level + STEPS + c] for c in range(STEPS)]
    cols = []
    for j in range(8):
        col = jnp.zeros(shape, jnp.float32)
        for k in range(nodes):
            piece = gram_now[8 * k : 8 * k + 8, 8 * k + j : 8 * k + j + 1]
            col = jnp.where(lane == k, piece, col)
        cols.append(col)
    for _ in range(SUBITERS):
        image = []
        for c in range(STEPS):
            total = cols[0] * basis[c][0:1, :]
            for j in range(1, 8):
                total = total + cols[j] * basis[c][j : j + 1, :]
            image.append(total * live[c])
        inner = {}
        for a in range(STEPS):
            for b in range(a + 1):
                inner[a, b] = sublane_sum(image[a] * image[b])
            inner[a, a] = inner[a, a] + (1.0 - live[a])
        low = {}
        inv = []
        for b in range(STEPS):
            pivot = inner[b, b]
            for k in range(b):
                pivot = pivot - low[b, k] * low[b, k]
            root = lax.rsqrt(pivot)
            root = root * (1.5 - 0.5 * pivot * root * root)
            inv.append(root)
            for a in range(b + 1, STEPS):
                entry = inner[a, b]
                for k in range(b):
                    entry = entry - low[a, k] * low[b, k]
                low[a, b] = entry * root
        fresh = []
        for a in range(STEPS):
            value = image[a]
            for k in range(a):
                value = value - low[a, k] * fresh[k]
            fresh.append(value * inv[a])
        basis = fresh
    return basis


def weights(basis, nodes):
    lane = lane_iota((8, 128))
    rows = []
    for k in range(nodes):
        block = jnp.zeros((8, 128), jnp.float32)
        for c in range(STEPS):
            block = jnp.where(lane == STEPS * k + c, basis[c][:, k : k + 1], block)
        rows.append(block)
    return jnp.concatenate(rows, axis=0) if nodes > 1 else rows[0]


def finish_kernel(start_ref, part_ref, *refs):
    out_ref, w_ref = refs[-2:]
    cores = refs[:STEPS]
    packed = part_ref[0]
    for i in range(1, part_ref.shape[0]):
        packed = packed + part_ref[i]
    size = RUNS * STEPS
    raw = jnp.concatenate(
        [packed if j == 0 else pltpu.roll(packed, 128 - size * j, 1) for j in range(STEPS)], axis=0
    )
    sub = sub_iota((size, 128))
    lane = lane_iota((size, 128))
    raw = jnp.where(lane < size, raw, 0.0)
    eight = sub_iota((8, 128))
    blocks = []
    for m in range(STEPS):
        block = jnp.zeros((8, 128), jnp.float32)
        for r in range(8):
            at = 8 * (r & 3) + 2 * m + (r >> 2)
            block = jnp.where(eight == r, raw[at : at + 1, :], block)
        blocks.append(block)
    full = jnp.concatenate(blocks, axis=0)
    square = jnp.concatenate([full, jnp.zeros((128 - size, 128), jnp.float32)], axis=0)
    mirror = square.T[:size, :]
    same = ((sub & 3) == (lane & 3)) & (((lane & 16) == 0) | ((sub & 16) != 0))
    full = jnp.where(((sub & 3) < (lane & 3)) | same, full, mirror)
    diag = jnp.where(sub == lane, full, 0.0)
    mu_col = jnp.sum(diag, axis=1, keepdims=True) / CELLS
    mu_row = jnp.sum(diag, axis=0, keepdims=True) / CELLS
    scale_col = 1.0 / jnp.sqrt(mu_col + EPS)
    scale_row = 1.0 / jnp.sqrt(mu_row + EPS)
    gram_now = full * scale_col * scale_row / CELLS
    nodes = RUNS // 2
    level = 0
    total = None
    while nodes:
        basis = level_basis(gram_now, nodes, level, start_ref)
        w = weights(basis, nodes)
        rows_now = 8 * nodes
        total = w if total is None else dot(total[:, :rows_now], w)
        if nodes > 1:
            half = dot(gram_now[:, :rows_now], w)
            rows = []
            for b in range(nodes // 2):
                block = jnp.zeros((8, 128), jnp.float32)
                for r in range(8):
                    k = 2 * b + (r >> 2)
                    column = basis[r & 3][:, k : k + 1]
                    row = sublane_sum(column * half[8 * k : 8 * k + 8, :])
                    block = jnp.where(eight == r, row, block)
                rows.append(block)
            gram_now = jnp.concatenate(rows, axis=0) if len(rows) > 1 else rows[0]
        level += 1
        nodes //= 2
    total = total * scale_col
    for c in range(STEPS):
        w_ref[c] = jnp.broadcast_to(total[:, c : c + 1], (size, 128))
    tiles = [slice(8 * i, 8 * i + 8) for i in range(BLOCK // 8)]
    for l in range(NZ // 128):
        cols = slice(128 * l, 128 * l + 128)
        accs = [[None] * len(tiles) for _ in range(STEPS)]
        for q in range(RUNS):
            for t in range(STEPS):
                k = STEPS * q + t
                xs = [cores[t][q, rows, cols] for rows in tiles]
                for c in range(STEPS):
                    weight = jnp.broadcast_to(w_ref[c, k : k + 1, :], (8, 128))
                    for i, x in enumerate(xs):
                        term = weight * x
                        accs[c][i] = term if accs[c][i] is None else accs[c][i] + term
        for c in range(STEPS):
            for i, rows in enumerate(tiles):
                out_ref[c, 0, rows, cols] = accs[c][i]


def finish(start, parts, cores):
    return pl.pallas_call(
        finish_kernel,
        out_shape=jax.ShapeDtypeStruct((STEPS, 1, BLOCK, NZ), jnp.float32),
        in_specs=[VMEM] * (2 + STEPS),
        out_specs=VMEM,
        scratch_shapes=[pltpu.VMEM((STEPS, RUNS * STEPS, 128), jnp.float32)],
        compiler_params=params(),
        cost_estimate=pl.CostEstimate(flops=5000000, bytes_accessed=2400000, transcendentals=0),
        name="finish",
    )(start, parts, *cores)


def local(start_field, viscosity, diffusivity, velocity, assignment, child_order, keep_ranks):
    sibling = [(i, i ^ 1) for i in range(NX)]
    crossing = [(i, i + 1) for i in range(1, NX - 1, 2)] + [(i + 1, i) for i in range(1, NX - 1, 2)]
    blocks = lax.all_to_all(row_blocks(start_field), "run", 0, 0)
    own = assemble(blocks, viscosity)
    table = run_rates(diffusivity, velocity, assignment)
    start = starts(child_order, keep_ranks)
    planes = None
    cores = []
    packed = None

    def swap_cross(a):
        return lax.ppermute(a, SPACE, crossing)

    def swap_sib(a):
        return lax.ppermute(a, SPACE, sibling)

    for turn in range(STEPS // 2):
        sib1 = swap_sib(own)
        cross1 = swap_cross(own)
        if planes is None:
            v, vs1, vc1 = own, sib1, cross1
        acc_own = interior(own, v, table)
        acc_sib = interior(sib1, vs1, table)
        last = turn == STEPS // 2 - 1
        cross2 = swap_cross(sib1)
        if cores:
            early = (cross1, packed, acc_own, acc_sib)
            cross1, packed, acc_own, acc_sib = lax.optimization_barrier(early)
        else:
            early = (cross1, acc_own, acc_sib, start)
            cross1, acc_own, acc_sib, start = lax.optimization_barrier(early)
        sib2 = swap_sib(trim(cross1) if last else cross1)
        if planes is None:
            planes = vs2, vc2 = sib2, cross2
        acc_cross = interior(cross1, vc1, table)
        fresh, core = close(("full", "core"), acc_own, own, sib1, cross1, v, vs1, vc1, table)
        cores.append(core)
        packed = gram(cores, packed, False)
        (near_sib,) = close(("full",), acc_sib, sib1, sib2, own, vs1, vs2, v, table)
        acc_own = interior(fresh, v, table)
        (near_cross,) = close(("full",), acc_cross, cross1, own, cross2, vc1, v, vc2, table, edge=True)
        want = ("core",) if last else ("full", "core")
        result = close(want, acc_own, fresh, near_sib, near_cross, v, vs1, vc1, table)
        cores.append(result[-1])
        own = result[0]
        if not last:
            packed = gram(cores, packed, False)
    parts = gram(cores, packed, True)
    parts = spread(lax.all_to_all(parts, ("y", "core"), 0, 0))
    parts = lax.all_to_all(parts, ("run", "x"), 0, 0)
    return finish(start, parts, cores)


def solution(mesh):
    fine = Mesh(mesh.devices.reshape(8, 4, 8, 2), ("run", "x", "y", "core"))
    in_specs = (P("run", SPACE, None, None), P(SPACE, None, None), P(), P(), P(), P(), P())
    out_specs = P(None, SPACE, "run", None)
    return jax.shard_map(local, mesh=fine, in_specs=in_specs, out_specs=out_specs, check_vma=False)
```
